128 devices in a mesh: seq: 16 (over z, x), head: 8 (over y, core).
Axes of the slice: x: 4, y: 4, z: 4, core: 2. Of those that a mesh axis runs over, the one named last changes fastest.
Arguments:
- tokens: bfloat16 [32768, 2048], P('seq'), may hold values from -6 to 6
- norm_gain: float32 [2048], replicated, may hold values from 0.5 to 2
- in_weight: bfloat16 [2048, 3, 2048], P(None, None, 'head')
- out_weight: bfloat16 [2048, 2048], P('head'), may hold values from -0.125 to 0.125
- pattern: int32 [256, 4], replicated, may hold values from 0 to 255, as said below
Outputs:
- mixed: bfloat16 [32768, 2048], P(('seq', 'head'))
The draws below stay inside these ranges and needn't reach their ends.
Inputs may be any that keep to these rules, and one draw needn't show every extreme that they name: `pattern`: row i names first tile i itself, then 4 - 1 distinct tiles held by other indices of seq (index = tile // 16). Among the rows of one index of seq, at most 4 of these later entries name tiles of any one other index, and every index has one such other index that it names exactly 4 times.
All inputs are finite; a program needn't handle non-finite values.
Results may differ from the reference program's by a relative error of at most 0.019.
Values may be sent and summed in bfloat16 or wider, within the bound.
No kernel may reach another device: no remote copies, remote signals or barrier semaphores. Data moves between devices by JAX's collectives and lax.ppermute only.
A program may use at most 128 MiB of HBM per device.

```python
import math
import jax
import jax.numpy as jnp
from jax import lax

D = 2048
H = 16
HD = 128
TILE = 128
KT = 4
SHARDS = 16
TOKENS = 32768
QT_DEV = 16
CAP = 4


def draw_in_weight(key, part):
    key_query, key_key, key_value = jax.random.split(key, 3)
    query_weight = jax.random.normal(key_query, (D, H * HD), jnp.float32) / jnp.sqrt(jnp.float32(D))
    value_weight = jax.random.normal(key_value, (D, H * HD), jnp.float32) / jnp.sqrt(jnp.float32(D))
    noise_weight = jax.random.normal(key_key, (D, H * HD), jnp.float32) / jnp.sqrt(jnp.float32(D))
    key_weight = noise_weight
    return jnp.stack([query_weight, key_weight, value_weight], axis=1).astype(jnp.bfloat16)


def draw_pattern(key, part):
    entries = QT_DEV * (KT - 1)
    slot_total = (SHARDS - 1) * CAP

    def for_device(device):
        device_key = jax.random.fold_in(key, device)
        key_hub, key_order, key_base = jax.random.split(device_key, 3)
        hub_offset = jax.random.randint(key_hub, (), 1, SHARDS)
        counter = jnp.arange(slot_total, dtype=jnp.int32)
        offsets = 1 + counter // CAP
        shuffled = jax.random.permutation(key_order, slot_total).astype(jnp.int32)
        ranking = jnp.where(offsets == hub_offset, -1 - counter % CAP, shuffled)
        order = jnp.argsort(ranking, stable=True)
        picked = offsets[order][:entries]
        owners = (device + picked) % SHARDS
        bases = jax.random.randint(key_base, (SHARDS,), 0, QT_DEV)
        position = jnp.arange(entries, dtype=jnp.int32)
        row_pos = position // (KT - 1)
        slot_pos = position % (KT - 1) + 1
        local_tile = (bases[owners] + row_pos + slot_pos) % QT_DEV
        remote = (owners * QT_DEV + local_tile).reshape(QT_DEV, KT - 1)
        own_tiles = device * QT_DEV + jnp.arange(QT_DEV, dtype=jnp.int32)
        return jnp.concatenate([own_tiles[:, None], remote], axis=1)
    table = jax.vmap(for_device)(jnp.arange(SHARDS, dtype=jnp.int32))
    return table.reshape(SHARDS * QT_DEV, KT).astype(jnp.int32)


def shard_levels(rng, shape, cuts, smallest, largest):
    factor_of = 1.0
    for axis_at, parts in cuts:
        steps = jax.random.uniform(jax.random.fold_in(jax.random.fold_in(rng, 6), axis_at), (parts,), jnp.float32, smallest / len(cuts), largest / len(cuts))
        factor_of = factor_of * jnp.repeat(jnp.exp(steps), shape[axis_at] // parts).reshape((-1,) + (1,) * (len(shape) - 1 - axis_at))
    return factor_of


def centred(key, shape, width, reach, pieces=(), held_as=jnp.bfloat16):
    drawn = width * jax.random.normal(key, shape, jnp.float32)
    if pieces:
        drawn = drawn * shard_levels(key, shape, pieces, -0.22, 0.18)
    return jnp.clip(drawn, -reach, reach).astype(held_as)


def setup_inputs(seed: int = 0) -> dict:
    arg_keys = jax.random.split(jax.random.key(seed), 6)
    return {
        "tokens": centred(arg_keys[0], (TOKENS, D), 1.0, 6.0, ((0, 16),)),
        "norm_gain": jnp.clip(jnp.exp(jax.random.uniform(arg_keys[1], (D,), jnp.float32, math.log(0.5), math.log(2.0))), 0.5, 2.0),
        "in_weight": draw_in_weight(jax.random.fold_in(arg_keys[5], 71), 0),
        "out_weight": centred(arg_keys[3], (H * HD, D), (H * HD) ** -0.5, 0.125, ((0, 8),)),
        "pattern": draw_pattern(jax.random.fold_in(arg_keys[5], 71), 0),
    }


def reference(tokens, norm_gain, in_weight, out_weight, pattern):
    values = tokens.astype(jnp.float32)
    mean_square = lax.optimization_barrier(jnp.mean(values * values, axis=-1, keepdims=True))
    normed = (values * lax.rsqrt(mean_square + 1e-05) * norm_gain).astype(jnp.bfloat16)
    projected = jnp.dot(normed, in_weight.reshape(D, 3 * H * HD), preferred_element_type=jnp.float32).astype(jnp.bfloat16)
    projected = lax.optimization_barrier(projected).reshape(TOKENS, 3, H, HD)
    tile_total = TOKENS // TILE
    query_tiles = projected[:, 0].reshape(tile_total, TILE, H, HD)
    key_tiles = projected[:, 1].reshape(tile_total, TILE, H, HD)
    value_tiles = projected[:, 2].reshape(tile_total, TILE, H, HD)
    scale = 1.0 / math.sqrt(HD)

    def one_tile(index):
        chosen = pattern[index]
        query_block = query_tiles[index].astype(jnp.float32)
        key_block = key_tiles[chosen].reshape(KT * TILE, H, HD).astype(jnp.float32)
        value_block = value_tiles[chosen].reshape(KT * TILE, H, HD).astype(jnp.float32)
        scores = jnp.einsum('qhd,khd->hqk', query_block, key_block) * scale
        maxima = lax.optimization_barrier(jnp.max(scores, axis=-1, keepdims=True))
        exponent = jnp.exp(scores - maxima)
        weights = (exponent / lax.optimization_barrier(jnp.sum(exponent, axis=-1, keepdims=True))).astype(jnp.bfloat16)
        weights = lax.optimization_barrier(weights).astype(jnp.float32)
        return jnp.einsum('hqk,khd->qhd', weights, value_block).astype(jnp.bfloat16)
    attended = lax.map(one_tile, jnp.arange(tile_total, dtype=jnp.int32)).reshape(TOKENS, H * HD)
    return jnp.dot(attended, out_weight, preferred_element_type=jnp.float32).astype(jnp.bfloat16)
```

```python
import functools
import math

import jax
import jax.numpy as jnp
from jax import lax
from jax.experimental import pallas as pl
from jax.experimental.pallas import tpu as pltpu
from jax.sharding import PartitionSpec as P

HD = 128
TILE = 128
KT = 4
CAP = 4
CHUNKS = 2
BLOCK = 256
GROUP = 4


def tables_kernel(me_ref, pattern_ref, chosen_ref, source_ref, *, shards, tiles):
    total = shards * tiles
    table = pattern_ref[...]
    owner = table // tiles
    local = table % tiles
    row = lax.broadcasted_iota(jnp.int32, (total, total), 0)
    col = lax.broadcasted_iota(jnp.int32, (total, total), 1)
    same = (row // tiles) == (col // tiles)
    every = same.astype(jnp.bfloat16)
    before = (same & (row < col)).astype(jnp.bfloat16)
    index = lax.broadcasted_iota(jnp.int32, (shards, total), 0)
    names = [(owner[c : c + 1] == index).astype(jnp.bfloat16) for c in range(1, KT)]
    dot = functools.partial(jnp.dot, preferred_element_type=jnp.float32)
    earlier = jnp.zeros((shards, total), jnp.float32)
    picked = [jnp.zeros((1, total), jnp.float32) for _ in range(CAP)]
    source_ref[0:1, :] = jnp.zeros((1, total), jnp.int32)
    for c in range(1, KT):
        here = names[c - 1]
        rank = jnp.sum(here.astype(jnp.float32) * (dot(here, before) + earlier), axis=0, keepdims=True)
        earlier = earlier + dot(here, every)
        rank = rank.astype(jnp.int32)
        mine = owner[c : c + 1] == me_ref[0]
        source_ref[c : c + 1, :] = owner[c : c + 1] * CAP + rank
        for k in range(CAP):
            picked[k] += jnp.where(mine & (rank == k), local[c : c + 1], 0).astype(jnp.float32)
    tile_row = lax.broadcasted_iota(jnp.int32, (total, 128), 0)
    lane = lax.broadcasted_iota(jnp.int32, (total, 128), 1)
    spread = ((tile_row // tiles) == lane).astype(jnp.bfloat16)
    for k in range(CAP):
        chosen_ref[k : k + 1, :] = dot(picked[k].astype(jnp.bfloat16), spread).astype(jnp.int32)


def project_kernel(chosen_ref, tokens_ref, gain_ref, weight_ref, queries_ref, *rest, shards, chunks):
    own_refs, send_refs = rest[:chunks], rest[chunks : 2 * chunks]
    held_refs, semaphore = rest[2 * chunks : 3 * chunks], rest[3 * chunks]
    step = pl.program_id(0)
    values = tokens_ref[...].astype(jnp.float32)
    mean_square = jnp.mean(values * values, axis=-1, keepdims=True)
    normed = (values * lax.rsqrt(mean_square + 1e-05) * gain_ref[...]).astype(jnp.bfloat16)
    parts = []
    for c in range(3):
        part = jnp.dot(normed, weight_ref[c], preferred_element_type=jnp.float32)
        parts.append(part.astype(jnp.bfloat16))
    count = BLOCK // TILE
    width = parts[0].shape[1] // chunks
    queries_ref[...] = parts[0].reshape(count, TILE, parts[0].shape[1])
    for h in range(chunks):
        keys = parts[1][:, h * width : (h + 1) * width].reshape(count, TILE, width)
        vals = parts[2][:, h * width : (h + 1) * width].reshape(count, TILE, width)
        own_refs[h][:, :, :width] = keys
        own_refs[h][:, :, width:] = vals
        held_refs[h][pl.ds(step * count, count), :, :width] = keys
        held_refs[h][pl.ds(step * count, count), :, width:] = vals

    @pl.when(step == pl.num_programs(0) - 1)
    def _():
        for h in range(chunks):
            for d in range(shards):
                for k in range(CAP):
                    pltpu.make_async_copy(
                        held_refs[h].at[chosen_ref[k, d]], send_refs[h].at[d, k], semaphore
                    ).start()
        for h in range(chunks):
            for d in range(shards):
                for k in range(CAP):
                    pltpu.make_async_copy(
                        held_refs[h].at[chosen_ref[k, d]], send_refs[h].at[d, k], semaphore
                    ).wait()


def attend_kernel(first_ref, source_ref, queries_ref, own_ref, *rest):
    remote_refs, out_ref = rest[:-1], rest[-1]
    width = queries_ref.shape[2]
    scale = 1.0 / math.sqrt(HD)
    for g in range(GROUP):
        blocks = [own_ref.at[g]] + [remote_refs[g * (KT - 1) + j].at[0] for j in range(KT - 1)]
        for h in range(width // HD):
            lanes = slice(h * HD, (h + 1) * HD)
            upper = slice(width + h * HD, width + (h + 1) * HD)
            query = queries_ref[g, :, lanes]
            scores = [
                lax.dot_general(
                    query, block[:, lanes], (((1,), (1,)), ((), ())), preferred_element_type=jnp.float32
                )
                for block in blocks
            ]
            highest = functools.reduce(jnp.maximum, scores)
            highest = jnp.max(highest, axis=-1, keepdims=True)
            exponents = [jnp.exp((s - highest) * scale) for s in scores]
            total = jnp.sum(functools.reduce(jnp.add, exponents), axis=-1, keepdims=True)
            attended = functools.reduce(
                jnp.add,
                [
                    jnp.dot(e.astype(jnp.bfloat16), block[:, upper], preferred_element_type=jnp.float32)
                    for e, block in zip(exponents, blocks)
                ],
            )
            out_ref[pl.ds(g * TILE, TILE), lanes] = (attended / total).astype(jnp.bfloat16)


def mix_kernel(*refs, chunks):
    attended_refs, weight_refs, out_ref = refs[:chunks], refs[chunks : 2 * chunks], refs[-1]
    total = None
    for attended_ref, weight_ref in zip(attended_refs, weight_refs):
        left = jnp.concatenate([attended_ref[s] for s in range(attended_ref.shape[0])], axis=1)
        right = weight_ref[...].reshape(left.shape[1], weight_ref.shape[3])
        part = jnp.dot(left, right, preferred_element_type=jnp.float32)
        total = part if total is None else total + part
    out_ref[...] = total.astype(jnp.bfloat16)


def body(tokens, norm_gain, in_weight, out_weight, pattern):
    shards = lax.axis_size("seq")
    groups = lax.axis_size("head")
    myself = lax.axis_index("seq")
    row_count, model = tokens.shape
    tiles = row_count // TILE
    head_width = in_weight.shape[2]
    chunks = CHUNKS
    width = head_width // chunks
    me = jnp.reshape(myself, (1,)).astype(jnp.int32)
    bf16 = jnp.bfloat16

    gathered = lax.all_gather(out_weight, "head", axis=0, tiled=True)

    smem = pl.BlockSpec(memory_space=pltpu.SMEM)
    chosen, source = pl.pallas_call(
        functools.partial(tables_kernel, shards=shards, tiles=tiles),
        in_specs=[smem, pl.BlockSpec(memory_space=pltpu.VMEM)],
        out_shape=[
            jax.ShapeDtypeStruct((8, 128), jnp.int32),
            jax.ShapeDtypeStruct((KT, shards * tiles), jnp.int32),
        ],
        name="tables",
    )(me, pattern.T)

    count = BLOCK // TILE
    outs = pl.pallas_call(
        functools.partial(project_kernel, shards=shards, chunks=chunks),
        grid_spec=pltpu.PrefetchScalarGridSpec(
            num_scalar_prefetch=1,
            grid=(row_count // BLOCK,),
            in_specs=[
                pl.BlockSpec((BLOCK, model), lambda i, c: (i, 0)),
                pl.BlockSpec((1, model), lambda i, c: (0, 0)),
                pl.BlockSpec((3, model, head_width), lambda i, c: (0, 0, 0), pipeline_mode=pl.Buffered(1)),
            ],
            out_specs=[pl.BlockSpec((count, TILE, head_width), lambda i, c: (i, 0, 0))]
            + [pl.BlockSpec((count, TILE, 2 * width), lambda i, c: (i, 0, 0))] * chunks
            + [pl.BlockSpec(memory_space=pl.ANY)] * chunks,
            scratch_shapes=[pltpu.VMEM((tiles, TILE, 2 * width), bf16)] * chunks + [pltpu.SemaphoreType.DMA],
        ),
        out_shape=[jax.ShapeDtypeStruct((tiles, TILE, head_width), bf16)]
        + [jax.ShapeDtypeStruct((tiles, TILE, 2 * width), bf16)] * chunks
        + [jax.ShapeDtypeStruct((shards, CAP, TILE, 2 * width), bf16)] * chunks,
        compiler_params=pltpu.CompilerParams(vmem_limit_bytes=48 * 1024 * 1024),
        name="project",
    )(chosen, tokens, norm_gain.reshape(1, model), in_weight.transpose(1, 0, 2))
    queries, owns, sends = outs[0], outs[1 : 1 + chunks], outs[1 + chunks :]

    first = me * tiles
    received = []
    for h in range(chunks):
        incoming = lax.all_to_all(sends[h], "seq", split_axis=0, concat_axis=0, tiled=True)
        incoming = incoming.reshape(shards * CAP, TILE, 2 * width)
        remote_specs = []
        for g in range(GROUP):
            for j in range(1, KT):
                remote_specs.append(
                    pl.BlockSpec(
                        (1, TILE, 2 * width),
                        lambda i, f, s, g=g, j=j: (s[j, f[0] + i * GROUP + g], 0, 0),
                    )
                )
        attended = pl.pallas_call(
            attend_kernel,
            grid_spec=pltpu.PrefetchScalarGridSpec(
                num_scalar_prefetch=2,
                grid=(tiles // GROUP,),
                in_specs=[
                    pl.BlockSpec((GROUP, TILE, width), lambda i, f, s, h=h: (i, 0, h)),
                    pl.BlockSpec((GROUP, TILE, 2 * width), lambda i, f, s: (i, 0, 0)),
                ]
                + remote_specs,
                out_specs=pl.BlockSpec((GROUP * TILE, width), lambda i, f, s: (i, 0)),
            ),
            out_shape=jax.ShapeDtypeStruct((row_count, width), bf16),
            name="attend",
        )(first, source, queries, owns[h], *([incoming] * len(remote_specs)))
        received.append(
            lax.all_to_all(
                attended.reshape(groups, row_count // groups, width), "head", split_axis=0, concat_axis=0, tiled=True
            )
        )

    rows = row_count // groups
    columns = 512
    weights = gathered.reshape(groups, chunks, width, model)
    return pl.pallas_call(
        functools.partial(mix_kernel, chunks=chunks),
        grid=(model // columns,),
        in_specs=[pl.BlockSpec((groups, rows, width), lambda i: (0, 0, 0))] * chunks
        + [
            pl.BlockSpec((groups, 1, width, columns), lambda i, h=h: (0, h, 0, i))
            for h in range(chunks)
        ],
        out_specs=pl.BlockSpec((rows, columns), lambda i: (0, i)),
        out_shape=jax.ShapeDtypeStruct((rows, model), bf16),
        compiler_params=pltpu.CompilerParams(vmem_limit_bytes=48 * 1024 * 1024),
        name="mix",
    )(*received, *([weights] * chunks))


def solution(mesh):
    return jax.shard_map(
        body,
        mesh=mesh,
        in_specs=(P("seq", None), P(), P(None, None, "head"), P("head", None), P()),
        out_specs=P(("seq", "head"), None),
        check_vma=False,
    )
```

```python
import functools
import math

import jax
import jax.numpy as jnp
from jax import lax
from jax.experimental import pallas as pl
from jax.experimental.pallas import tpu as pltpu
from jax.sharding import PartitionSpec as P

HD = 128
TILE = 128
KT = 4
CAP = 4
BLOCK = 512
GROUP = 4
PARTS = 8
VMEM = 48 * 1024 * 1024
MOST = 60 * 1024 * 1024


def tables_kernel(me_ref, pattern_ref, chosen_ref, source_ref, *, shards, tiles):
    total = shards * tiles
    table = pattern_ref[...]
    owner = table // tiles
    local = table % tiles
    row = lax.broadcasted_iota(jnp.int32, (total, total), 0)
    col = lax.broadcasted_iota(jnp.int32, (total, total), 1)
    same = (row // tiles) == (col // tiles)
    every = same.astype(jnp.bfloat16)
    before = (same & (row < col)).astype(jnp.bfloat16)
    index = lax.broadcasted_iota(jnp.int32, (shards, total), 0)
    names = [(owner[c : c + 1] == index).astype(jnp.bfloat16) for c in range(1, KT)]
    dot = functools.partial(jnp.dot, preferred_element_type=jnp.float32)
    earlier = jnp.zeros((shards, total), jnp.float32)
    picked = [jnp.zeros((1, total), jnp.float32) for _ in range(CAP)]
    source_ref[0:1, :] = jnp.zeros((1, total), jnp.int32)
    for c in range(1, KT):
        here = names[c - 1]
        rank = jnp.sum(here.astype(jnp.float32) * (dot(here, before) + earlier), axis=0, keepdims=True)
        earlier = earlier + dot(here, every)
        rank = rank.astype(jnp.int32)
        mine = owner[c : c + 1] == me_ref[0]
        source_ref[c : c + 1, :] = owner[c : c + 1] * CAP + rank
        for k in range(CAP):
            picked[k] += jnp.where(mine & (rank == k), local[c : c + 1], 0).astype(jnp.float32)
    tile_row = lax.broadcasted_iota(jnp.int32, (total, 128), 0)
    lane = lax.broadcasted_iota(jnp.int32, (total, 128), 1)
    spread = ((tile_row // tiles) == lane).astype(jnp.bfloat16)
    for k in range(CAP):
        chosen_ref[k : k + 1, :] = dot(picked[k].astype(jnp.bfloat16), spread).astype(jnp.int32)


def project_kernel(*refs, widths, scales):
    count = len(widths)
    tokens_ref, gain_ref = refs[0], refs[1]
    weight_refs = refs[2 : 2 + count]
    out_refs = refs[2 + count : 2 + count + scales]
    scaled_ref = refs[-1]
    model = scaled_ref.shape[0]
    step = pl.program_id(0)

    @pl.when(step == 0)
    def _():
        gains = jnp.transpose(gain_ref[...])
        for j in range(model // HD):
            rows = slice(j * HD, (j + 1) * HD)
            at = 0
            for ref, width in zip(weight_refs, widths):
                part = ref[0, rows, :].astype(jnp.float32) * gains[:, j : j + 1]
                scaled_ref[rows, at : at + width] = part.astype(jnp.bfloat16)
                at += width

    tokens = tokens_ref[...]
    values = tokens.astype(jnp.float32)
    inverse = lax.rsqrt(jnp.mean(values * values, axis=-1, keepdims=True) + 1e-05)
    result = jnp.dot(tokens, scaled_ref[...], preferred_element_type=jnp.float32) * inverse
    result = result.astype(jnp.bfloat16)
    at = 0
    for ref in out_refs:
        width = ref.shape[2]
        ref[...] = result[:, at : at + width].reshape(ref.shape)
        at += width


def project(tokens, gain, weights, columns, outs):
    rows, model = tokens.shape
    tiles, count = rows // TILE, BLOCK // TILE
    widths = [n * HD for _, _, n in columns]
    return pl.pallas_call(
        functools.partial(project_kernel, widths=widths, scales=len(outs)),
        grid=(rows // BLOCK,),
        in_specs=[
            pl.BlockSpec((BLOCK, model), lambda i: (i, 0)),
            pl.BlockSpec(gain.shape, lambda i: (0, 0)),
        ]
        + [
            pl.BlockSpec((1, model, n * HD), lambda i, c=c, b=b: (c, 0, b), pipeline_mode=pl.Buffered(1))
            for c, b, n in columns
        ],
        out_specs=[pl.BlockSpec((count, TILE, width), lambda i: (i, 0, 0)) for width in outs],
        out_shape=[jax.ShapeDtypeStruct((tiles, TILE, width), jnp.bfloat16) for width in outs],
        scratch_shapes=[pltpu.VMEM((model, sum(widths)), jnp.bfloat16)],
        compiler_params=pltpu.CompilerParams(vmem_limit_bytes=MOST),
        name="project",
    )(tokens, gain, *([weights] * len(columns)))


def dispatch_kernel(chosen_ref, held_ref, send_ref, staged, semaphores, *, shards):
    copies = []
    for part in range(PARTS):
        owners = shards // PARTS
        for d in range(part * owners, (part + 1) * owners):
            for k in range(CAP):
                staged[d, k] = held_ref[chosen_ref[k, d]]
        span = pl.ds(part * owners, owners)
        copy = pltpu.make_async_copy(staged.at[span], send_ref.at[span], semaphores.at[part])
        copy.start()
        copies.append(copy)
    for copy in copies:
        copy.wait()


def dispatch(chosen, held, shards):
    shape = (shards, CAP) + held.shape[1:]
    return pl.pallas_call(
        functools.partial(dispatch_kernel, shards=shards),
        in_specs=[pl.BlockSpec(memory_space=pltpu.SMEM), pl.BlockSpec(memory_space=pltpu.VMEM)],
        out_specs=pl.BlockSpec(memory_space=pltpu.HBM),
        out_shape=jax.ShapeDtypeStruct(shape, held.dtype),
        scratch_shapes=[pltpu.VMEM(shape, held.dtype), pltpu.SemaphoreType.DMA((PARTS,))],
        compiler_params=pltpu.CompilerParams(vmem_limit_bytes=MOST),
        name="dispatch",
    )(chosen, held)


def attend_kernel(first_ref, source_ref, queries_ref, own_ref, incoming_ref, out_ref, held, semaphores, *, tiles):
    share = held.shape[0] // PARTS
    copies = []
    for part in range(PARTS):
        span = pl.ds(part * share, share)
        copies.append(pltpu.make_async_copy(incoming_ref.at[span], held.at[span], semaphores.at[part]))
        copies[-1].start()
    for copy in copies:
        copy.wait()
    scale = 1.0 / math.sqrt(HD) * math.log2(math.e)
    for start in range(0, tiles, GROUP):
        group = range(start, start + GROUP)
        blocks = [
            [own_ref.at[i]] + [held.at[source_ref[j, first_ref[0] + i]] for j in range(1, KT)] for i in group
        ]
        scores = [
            [
                lax.dot_general(
                    queries_ref[i], b[:, :HD], (((1,), (1,)), ((), ())), preferred_element_type=jnp.float32
                )
                for b in bs
            ]
            for i, bs in zip(group, blocks)
        ]
        highest = [jnp.max(functools.reduce(jnp.maximum, s), axis=-1, keepdims=True) * scale for s in scores]
        exponents = [[jnp.exp2(x * scale - m) for x in s] for s, m in zip(scores, highest)]
        totals = [jnp.sum(functools.reduce(jnp.add, e), axis=-1, keepdims=True) for e in exponents]
        for i, e, total, bs in zip(group, exponents, totals, blocks):
            weights = jnp.concatenate([x.astype(jnp.bfloat16) for x in e], axis=1)
            values = jnp.concatenate([b[:, HD:] for b in bs], axis=0)
            attended = jnp.dot(weights, values, preferred_element_type=jnp.float32)
            out_ref[i * TILE : (i + 1) * TILE, :] = (attended * (1.0 / total)).astype(jnp.bfloat16)


def attend(first, source, queries, own, incoming):
    tiles = own.shape[0]
    vmem, smem = pl.BlockSpec(memory_space=pltpu.VMEM), pl.BlockSpec(memory_space=pltpu.SMEM)
    return pl.pallas_call(
        functools.partial(attend_kernel, tiles=tiles),
        in_specs=[smem, smem, vmem, vmem, pl.BlockSpec(memory_space=pl.ANY)],
        out_specs=vmem,
        out_shape=jax.ShapeDtypeStruct((tiles * TILE, HD), jnp.bfloat16),
        scratch_shapes=[pltpu.VMEM(incoming.shape, jnp.bfloat16), pltpu.SemaphoreType.DMA((PARTS,))],
        compiler_params=pltpu.CompilerParams(vmem_limit_bytes=VMEM),
        name="attend",
    )(first, source, queries, own, incoming)


def mix_kernel(*refs, chunks):
    attended_refs, weight_refs, out_ref = refs[:chunks], refs[chunks : 2 * chunks], refs[-1]
    total = None
    for attended_ref, weight_ref in zip(attended_refs, weight_refs):
        left = jnp.concatenate([attended_ref[s] for s in range(attended_ref.shape[0])], axis=1)
        right = weight_ref[...].reshape(left.shape[1], weight_ref.shape[3])
        part = jnp.dot(left, right, preferred_element_type=jnp.float32)
        total = part if total is None else total + part
    out_ref[...] = total.astype(jnp.bfloat16)


def body(tokens, norm_gain, in_weight, out_weight, pattern):
    shards = lax.axis_size("seq")
    groups = lax.axis_size("head")
    myself = lax.axis_index("seq")
    row_count, model = tokens.shape
    tiles = row_count // TILE
    heads = in_weight.shape[2] // HD
    me = jnp.reshape(myself, (1,)).astype(jnp.int32)

    gathered = lax.all_gather(out_weight, "head", axis=0, tiled=True)

    chosen, source = pl.pallas_call(
        functools.partial(tables_kernel, shards=shards, tiles=tiles),
        in_specs=[pl.BlockSpec(memory_space=pltpu.SMEM), pl.BlockSpec(memory_space=pltpu.VMEM)],
        out_shape=[
            jax.ShapeDtypeStruct((8, 128), jnp.int32),
            jax.ShapeDtypeStruct((KT, shards * tiles), jnp.int32),
        ],
        name="tables",
    )(me, pattern.T)

    gain = norm_gain.reshape(model // HD, HD)
    weights = in_weight.transpose(1, 0, 2)
    queries, owns, incoming = [], [], []
    for h in range(heads):
        if h == 0:
            (own,) = project(tokens, gain, weights, [(1, h, 1), (2, h, 1)], [2 * HD])
        else:
            columns = [(1, h, 1), (2, h, 1)] + ([(0, 0, heads)] if h == 1 else [])
            outs = project(tokens, gain, weights, columns, [2 * HD] + [HD] * (heads if h == 1 else 0))
            own, queries = outs[0], queries + list(outs[1:])
        owns.append(own)
        send = dispatch(chosen, own, shards)
        send, tokens = lax.optimization_barrier((send, tokens))
        arrived = lax.all_to_all(send, "seq", split_axis=0, concat_axis=0, tiled=True)
        incoming.append(arrived.reshape(shards * CAP, TILE, 2 * HD))

    received = []
    for h in range(heads):
        attended = attend(me * tiles, source, queries[h], owns[h], incoming[h])
        received.append(
            lax.all_to_all(
                attended.reshape(groups, row_count // groups, HD), "head", split_axis=0, concat_axis=0, tiled=True
            )
        )

    rows = row_count // groups
    columns = 1024
    weights = gathered.reshape(groups, heads, HD, model)
    return pl.pallas_call(
        functools.partial(mix_kernel, chunks=heads),
        grid=(model // columns,),
        in_specs=[pl.BlockSpec((groups, rows, HD), lambda i: (0, 0, 0))] * heads
        + [pl.BlockSpec((groups, 1, HD, columns), lambda i, h=h: (0, h, 0, i)) for h in range(heads)],
        out_specs=pl.BlockSpec((rows, columns), lambda i: (0, i)),
        out_shape=jax.ShapeDtypeStruct((rows, model), jnp.bfloat16),
        compiler_params=pltpu.CompilerParams(vmem_limit_bytes=VMEM),
        name="mix",
    )(*received, *([weights] * heads))


def solution(mesh):
    return jax.shard_map(
        body,
        mesh=mesh,
        in_specs=(P("seq", None), P(), P(None, None, "head"), P("head", None), P()),
        out_specs=P(("seq", "head"), None),
        check_vma=False,
    )
```

```python
import functools
import math

import jax
import jax.numpy as jnp
from jax import lax
from jax.experimental import pallas as pl
from jax.experimental.pallas import tpu as pltpu
from jax.sharding import PartitionSpec as P

HD = 128
TILE = 128
KT = 4
CAP = 4
BLOCK = 512
GROUP = 2
SIDE = 4
SHIFTS = (10, 6, 12, 14, 4, 9, 3, 11, 1, 5, 15, 7, 13, 2, 8)
FLIGHT = 5
QUERIES_AFTER = 4
VMEM = 48 * 1024 * 1024
MOST = 60 * 1024 * 1024


def shift_of(source, target):
    rows = (target // SIDE - source // SIDE + SIDE) % SIDE
    return rows * SIDE + (target % SIDE - source % SIDE + SIDE) % SIDE


def shifted(source, shift):
    return (source // SIDE + shift // SIDE) % SIDE * SIDE + (source % SIDE + shift % SIDE) % SIDE


def tables_kernel(me_ref, pattern_ref, chosen_ref, source_ref, *, shards, tiles):
    total = shards * tiles
    table = pattern_ref[...]
    owner = table // tiles
    local = table % tiles
    row = lax.broadcasted_iota(jnp.int32, (total, total), 0)
    col = lax.broadcasted_iota(jnp.int32, (total, total), 1)
    same = (row // tiles) == (col // tiles)
    every = same.astype(jnp.bfloat16)
    before = (same & (row < col)).astype(jnp.bfloat16)
    index = lax.broadcasted_iota(jnp.int32, (shards, total), 0)
    names = [(owner[c : c + 1] == index).astype(jnp.bfloat16) for c in range(1, KT)]
    dot = functools.partial(jnp.dot, preferred_element_type=jnp.float32)
    earlier = jnp.zeros((shards, total), jnp.float32)
    picked = [jnp.zeros((1, total), jnp.float32) for _ in range(CAP)]
    source_ref[0:1, :] = jnp.zeros((1, total), jnp.int32)
    for c in range(1, KT):
        here = names[c - 1]
        rank = jnp.sum(here.astype(jnp.float32) * (dot(here, before) + earlier), axis=0, keepdims=True)
        earlier = earlier + dot(here, every)
        rank = rank.astype(jnp.int32)
        mine = owner[c : c + 1] == me_ref[0]
        source_ref[c : c + 1, :] = shift_of(owner[c : c + 1], me_ref[0]) * CAP + rank
        for k in range(CAP):
            picked[k] += jnp.where(mine & (rank == k), local[c : c + 1], 0).astype(jnp.float32)
    tile_row = lax.broadcasted_iota(jnp.int32, (total, 128), 0)
    lane = lax.broadcasted_iota(jnp.int32, (total, 128), 1)
    spread = ((tile_row // tiles) == lane).astype(jnp.bfloat16)
    for k in range(CAP):
        chosen_ref[k : k + 1, :] = dot(picked[k].astype(jnp.bfloat16), spread).astype(jnp.int32)


def project_kernel(*refs, widths, scales):
    count = len(widths)
    tokens_ref, gain_ref = refs[0], refs[1]
    weight_refs = refs[2 : 2 + count]
    out_refs = refs[2 + count : 2 + count + scales]
    scaled_ref = refs[-1]
    model = scaled_ref.shape[0]
    step = pl.program_id(0)

    @pl.when(step == 0)
    def _():
        gains = jnp.transpose(gain_ref[...])
        for j in range(model // HD):
            rows = slice(j * HD, (j + 1) * HD)
            at = 0
            for ref, width in zip(weight_refs, widths):
                part = ref[0, rows, :].astype(jnp.float32) * gains[:, j : j + 1]
                scaled_ref[rows, at : at + width] = part.astype(jnp.bfloat16)
                at += width

    tokens = tokens_ref[...]
    values = tokens.astype(jnp.float32)
    inverse = lax.rsqrt(jnp.mean(values * values, axis=-1, keepdims=True) + 1e-05)
    result = jnp.dot(tokens, scaled_ref[...], preferred_element_type=jnp.float32) * inverse
    result = result.astype(jnp.bfloat16)
    at = 0
    for ref in out_refs:
        width = ref.shape[2]
        ref[...] = result[:, at : at + width].reshape(ref.shape)
        at += width


def project(tokens, gain, weights, columns, outs):
    rows, model = tokens.shape
    tiles, count = rows // TILE, BLOCK // TILE
    widths = [n * HD for _, _, n in columns]
    return pl.pallas_call(
        functools.partial(project_kernel, widths=widths, scales=len(outs)),
        grid=(rows // BLOCK,),
        in_specs=[
            pl.BlockSpec((BLOCK, model), lambda i: (i, 0)),
            pl.BlockSpec(gain.shape, lambda i: (0, 0)),
        ]
        + [
            pl.BlockSpec((1, model, n * HD), lambda i, c=c, b=b: (c, 0, b), pipeline_mode=pl.Buffered(1))
            for c, b, n in columns
        ],
        out_specs=[pl.BlockSpec((count, TILE, width), lambda i: (i, 0, 0)) for width in outs],
        out_shape=[jax.ShapeDtypeStruct((tiles, TILE, width), jnp.bfloat16) for width in outs],
        scratch_shapes=[pltpu.VMEM((model, sum(widths)), jnp.bfloat16)],
        compiler_params=pltpu.CompilerParams(vmem_limit_bytes=MOST),
        name="project",
    )(tokens, gain, *([weights] * len(columns)))


def dispatch_kernel(me_ref, chosen_ref, held_ref, *rest, shifts):
    send_refs, staged, semaphores = rest[:-2], rest[-2], rest[-1]
    copies = []
    for p, shift in enumerate(shifts):
        target = shifted(me_ref[0], shift)
        for k in range(CAP):
            staged[p, k] = held_ref[chosen_ref[k, target]]
        copies.append(pltpu.make_async_copy(staged.at[p], send_refs[p], semaphores.at[p]))
        copies[-1].start()
    for copy in copies:
        copy.wait()


def dispatch(me, chosen, held, shifts):
    shape = (CAP,) + held.shape[1:]
    smem = pl.BlockSpec(memory_space=pltpu.SMEM)
    return pl.pallas_call(
        functools.partial(dispatch_kernel, shifts=shifts),
        in_specs=[smem, smem, pl.BlockSpec(memory_space=pltpu.VMEM)],
        out_specs=[pl.BlockSpec(memory_space=pltpu.HBM)] * len(shifts),
        out_shape=[jax.ShapeDtypeStruct(shape, held.dtype)] * len(shifts),
        scratch_shapes=[
            pltpu.VMEM((len(shifts),) + shape, held.dtype),
            pltpu.SemaphoreType.DMA((len(shifts),)),
        ],
        compiler_params=pltpu.CompilerParams(vmem_limit_bytes=MOST),
        name="dispatch",
    )(me, chosen, held)


def attend_kernel(first_ref, source_ref, queries_ref, own_ref, *rest, tiles, heads):
    incoming_refs, out_ref, held, semaphores = rest[:-3], rest[-3], rest[-2], rest[-1]
    copies = []
    for p, shift in enumerate(SHIFTS):
        copies.append(
            pltpu.make_async_copy(incoming_refs[p], held.at[pl.ds(shift * CAP, CAP)], semaphores.at[p])
        )
        copies[-1].start()
    for copy in copies:
        copy.wait()
    scale = 1.0 / math.sqrt(HD) * math.log2(math.e)
    for start in range(0, tiles, GROUP):
        group = range(start, start + GROUP)
        blocks = [
            [own_ref.at[i]] + [held.at[source_ref[j, first_ref[0] + i]] for j in range(1, KT)] for i in group
        ]
        pairs = [(i, bs, h) for i, bs in zip(group, blocks) for h in range(heads)]
        scores = [
            [
                lax.dot_general(
                    queries_ref[i, :, h * HD : (h + 1) * HD],
                    b[:, h * HD : (h + 1) * HD],
                    (((1,), (1,)), ((), ())),
                    preferred_element_type=jnp.float32,
                )
                for b in bs
            ]
            for i, bs, h in pairs
        ]
        highest = [jnp.max(functools.reduce(jnp.maximum, s), axis=-1, keepdims=True) * scale for s in scores]
        exponents = [[jnp.exp2(x * scale - m) for x in s] for s, m in zip(scores, highest)]
        totals = [jnp.sum(functools.reduce(jnp.add, e), axis=-1, keepdims=True) for e in exponents]
        for (i, bs, h), e, total in zip(pairs, exponents, totals):
            weights = jnp.concatenate([x.astype(jnp.bfloat16) for x in e], axis=1)
            upper = slice((heads + h) * HD, (heads + h + 1) * HD)
            values = jnp.concatenate([b[:, upper] for b in bs], axis=0)
            attended = jnp.dot(weights, values, preferred_element_type=jnp.float32)
            out_ref[i * TILE : (i + 1) * TILE, h * HD : (h + 1) * HD] = (attended * (1.0 / total)).astype(
                jnp.bfloat16
            )


def attend(first, source, queries, own, incoming):
    tiles = own.shape[0]
    vmem, smem = pl.BlockSpec(memory_space=pltpu.VMEM), pl.BlockSpec(memory_space=pltpu.SMEM)
    return pl.pallas_call(
        functools.partial(attend_kernel, tiles=tiles, heads=queries.shape[2] // HD),
        in_specs=[smem, smem, vmem, vmem] + [pl.BlockSpec(memory_space=pl.ANY)] * len(incoming),
        out_specs=vmem,
        out_shape=jax.ShapeDtypeStruct((tiles * TILE, queries.shape[2]), jnp.bfloat16),
        scratch_shapes=[
            pltpu.VMEM((SIDE * SIDE * CAP,) + own.shape[1:], jnp.bfloat16),
            pltpu.SemaphoreType.DMA((len(incoming),)),
        ],
        compiler_params=pltpu.CompilerParams(vmem_limit_bytes=VMEM),
        name="attend",
    )(first, source, queries, own, *incoming)


def mix_kernel(attended_ref, weight_ref, out_ref):
    left = jnp.concatenate([attended_ref[s] for s in range(attended_ref.shape[0])], axis=1)
    out_ref[...] = jnp.dot(left, weight_ref[...], preferred_element_type=jnp.float32).astype(jnp.bfloat16)


def body(tokens, norm_gain, in_weight, out_weight, pattern):
    shards = lax.axis_size("seq")
    groups = lax.axis_size("head")
    myself = lax.axis_index("seq")
    row_count, model = tokens.shape
    tiles = row_count // TILE
    width = in_weight.shape[2]
    heads = width // HD
    me = jnp.reshape(myself, (1,)).astype(jnp.int32)

    gathered = lax.all_gather(out_weight, "head", axis=0, tiled=True)

    chosen, source = pl.pallas_call(
        functools.partial(tables_kernel, shards=shards, tiles=tiles),
        in_specs=[pl.BlockSpec(memory_space=pltpu.SMEM), pl.BlockSpec(memory_space=pltpu.VMEM)],
        out_shape=[
            jax.ShapeDtypeStruct((8, 128), jnp.int32),
            jax.ShapeDtypeStruct((KT, shards * tiles), jnp.int32),
        ],
        name="tables",
    )(me, pattern.T)

    gain = norm_gain.reshape(model // HD, HD)
    weights = in_weight.transpose(1, 0, 2)
    (own,) = project(tokens, gain, weights, [(1, 0, heads), (2, 0, heads)], [2 * width])
    sends = list(dispatch(me, chosen, own, SHIFTS[:FLIGHT]))
    incoming = []
    for p, shift in enumerate(SHIFTS):
        if p == FLIGHT:
            held, incoming[0] = lax.optimization_barrier((own, incoming[0]))
            sends += list(dispatch(me, chosen, held, SHIFTS[FLIGHT:]))
        send = sends[p]
        if p >= FLIGHT:
            send, incoming[p - FLIGHT] = lax.optimization_barrier((send, incoming[p - FLIGHT]))
        incoming.append(lax.ppermute(send, "seq", [(s, shifted(s, shift)) for s in range(shards)]))
    tokens, incoming[QUERIES_AFTER] = lax.optimization_barrier((tokens, incoming[QUERIES_AFTER]))
    (queries,) = project(tokens, gain, weights, [(0, 0, heads)], [width])
    attended = attend(me * tiles, source, queries, own, incoming)
    rows = row_count // groups
    attended = lax.all_to_all(
        attended.reshape(groups, rows, width), "head", split_axis=0, concat_axis=0, tiled=True
    )
    columns = 1024
    return pl.pallas_call(
        mix_kernel,
        grid=(model // columns,),
        in_specs=[
            pl.BlockSpec((groups, rows, width), lambda i: (0, 0, 0)),
            pl.BlockSpec((groups * width, columns), lambda i: (0, i)),
        ],
        out_specs=pl.BlockSpec((rows, columns), lambda i: (0, i)),
        out_shape=jax.ShapeDtypeStruct((rows, model), jnp.bfloat16),
        compiler_params=pltpu.CompilerParams(vmem_limit_bytes=VMEM),
        name="mix",
    )(attended, gathered)


def solution(mesh):
    return jax.shard_map(
        body,
        mesh=mesh,
        in_specs=(P("seq", None), P(), P(None, None, "head"), P("head", None), P()),
        out_specs=P(("seq", "head"), None),
        check_vma=False,
    )
```

```python
import functools
import math

import jax
import jax.numpy as jnp
from jax import lax
from jax.experimental import pallas as pl
from jax.experimental.pallas import tpu as pltpu
from jax.sharding import PartitionSpec as P

HD = 128
TILE = 128
KT = 4
CAP = 4
BLOCK = 512
GROUP = 2
SIDE = 4
SHIFTS = (10, 6, 12, 14, 4, 3, 11, 1, 5, 15, 9, 7, 13, 2, 8)
LATE = 10
COLUMNS = 1024
VMEM = 60 * 1024 * 1024
MOST = 60 * 1024 * 1024
LEAST = 16 * 1024 * 1024


def shift_of(source, target):
    rows = (target // SIDE - source // SIDE + SIDE) % SIDE
    return rows * SIDE + (target % SIDE - source % SIDE + SIDE) % SIDE


def shifted(source, shift):
    return (source // SIDE + shift // SIDE) % SIDE * SIDE + (source % SIDE + shift % SIDE) % SIDE


def tables_kernel(me_ref, pattern_ref, chosen_ref, source_ref, *, shards, tiles):
    total = shards * tiles
    table = pattern_ref[...]
    owner = table // tiles
    local = table % tiles
    row = lax.broadcasted_iota(jnp.int32, (total, total), 0)
    col = lax.broadcasted_iota(jnp.int32, (total, total), 1)
    same = (row // tiles) == (col // tiles)
    every = same.astype(jnp.bfloat16)
    before = (same & (row < col)).astype(jnp.bfloat16)
    index = lax.broadcasted_iota(jnp.int32, (shards, total), 0)
    names = [(owner[c : c + 1] == index).astype(jnp.bfloat16) for c in range(1, KT)]
    dot = functools.partial(jnp.dot, preferred_element_type=jnp.float32)
    earlier = jnp.zeros((shards, total), jnp.float32)
    picked = [jnp.zeros((1, total), jnp.float32) for _ in range(CAP)]
    source_ref[0:1, :] = jnp.zeros((1, total), jnp.int32)
    for c in range(1, KT):
        here = names[c - 1]
        rank = jnp.sum(here.astype(jnp.float32) * (dot(here, before) + earlier), axis=0, keepdims=True)
        earlier = earlier + dot(here, every)
        rank = rank.astype(jnp.int32)
        mine = owner[c : c + 1] == me_ref[0]
        source_ref[c : c + 1, :] = shift_of(owner[c : c + 1], me_ref[0]) * CAP + rank
        for k in range(CAP):
            picked[k] += jnp.where(mine & (rank == k), local[c : c + 1], 0).astype(jnp.float32)
    tile_row = lax.broadcasted_iota(jnp.int32, (total, 128), 0)
    lane = lax.broadcasted_iota(jnp.int32, (total, 128), 1)
    spread = ((tile_row // tiles) == lane).astype(jnp.bfloat16)
    for k in range(CAP):
        chosen_ref[k : k + 1, :] = dot(picked[k].astype(jnp.bfloat16), spread).astype(jnp.int32)


def project_kernel(*refs, widths, scales):
    count = len(widths)
    tokens_ref, gain_ref = refs[0], refs[1]
    weight_refs = refs[2 : 2 + count]
    out_refs = refs[2 + count : 2 + count + scales]
    scaled_ref = refs[-1]
    model = scaled_ref.shape[0]
    step = pl.program_id(0)

    @pl.when(step == 0)
    def _():
        gains = jnp.transpose(gain_ref[...])
        for j in range(model // HD):
            rows = slice(j * HD, (j + 1) * HD)
            at = 0
            for ref, width in zip(weight_refs, widths):
                part = ref[0, rows, :].astype(jnp.float32) * gains[:, j : j + 1]
                scaled_ref[rows, at : at + width] = part.astype(jnp.bfloat16)
                at += width

    tokens = tokens_ref[...]
    values = tokens.astype(jnp.float32)
    inverse = lax.rsqrt(jnp.mean(values * values, axis=-1, keepdims=True) + 1e-05)
    result = jnp.dot(tokens, scaled_ref[...], preferred_element_type=jnp.float32) * inverse
    result = result.astype(jnp.bfloat16)
    at = 0
    for ref in out_refs:
        width = ref.shape[2]
        ref[...] = result[:, at : at + width].reshape(ref.shape)
        at += width


def project(tokens, gain, weights, columns, outs, limit):
    rows, model = tokens.shape
    tiles, count = rows // TILE, BLOCK // TILE
    widths = [n * HD for _, _, n in columns]
    return pl.pallas_call(
        functools.partial(project_kernel, widths=widths, scales=len(outs)),
        grid=(rows // BLOCK,),
        in_specs=[
            pl.BlockSpec((BLOCK, model), lambda i: (i, 0)),
            pl.BlockSpec(gain.shape, lambda i: (0, 0)),
        ]
        + [
            pl.BlockSpec((1, model, n * HD), lambda i, c=c, b=b: (c, 0, b), pipeline_mode=pl.Buffered(1))
            for c, b, n in columns
        ],
        out_specs=[pl.BlockSpec((count, TILE, width), lambda i: (i, 0, 0)) for width in outs],
        out_shape=[jax.ShapeDtypeStruct((tiles, TILE, width), jnp.bfloat16) for width in outs],
        scratch_shapes=[pltpu.VMEM((model, sum(widths)), jnp.bfloat16)],
        compiler_params=pltpu.CompilerParams(vmem_limit_bytes=limit),
        name="project",
    )(tokens, gain, *([weights] * len(columns)))


def dispatch_kernel(me_ref, chosen_ref, held_ref, *rest, shifts):
    send_refs, staged, semaphores = rest[:-2], rest[-2], rest[-1]
    copies = []
    for p, shift in enumerate(shifts):
        target = shifted(me_ref[0], shift)
        for k in range(CAP):
            staged[p, k] = held_ref[chosen_ref[k, target]]
        copies.append(pltpu.make_async_copy(staged.at[p], send_refs[p], semaphores.at[p]))
        copies[-1].start()
    for copy in copies:
        copy.wait()


def dispatch(me, chosen, held, shifts):
    shape = (CAP,) + held.shape[1:]
    smem = pl.BlockSpec(memory_space=pltpu.SMEM)
    return pl.pallas_call(
        functools.partial(dispatch_kernel, shifts=shifts),
        in_specs=[smem, smem, pl.BlockSpec(memory_space=pltpu.VMEM)],
        out_specs=[pl.BlockSpec(memory_space=pltpu.HBM)] * len(shifts),
        out_shape=[jax.ShapeDtypeStruct(shape, held.dtype)] * len(shifts),
        scratch_shapes=[
            pltpu.VMEM((len(shifts),) + shape, held.dtype),
            pltpu.SemaphoreType.DMA((len(shifts),)),
        ],
        compiler_params=pltpu.CompilerParams(vmem_limit_bytes=MOST),
        name="dispatch",
    )(me, chosen, held)


def attend_kernel(first_ref, source_ref, queries_ref, own_ref, *rest, tiles, heads, pairs):
    incoming_refs, out_refs, held, semaphores = rest[: -2 - pairs], rest[-2 - pairs : -2], rest[-2], rest[-1]
    copies = []
    for p, shift in enumerate(SHIFTS):
        copies.append(
            pltpu.make_async_copy(incoming_refs[p], held.at[pl.ds(shift * CAP, CAP)], semaphores.at[p])
        )
        copies[-1].start()
    for copy in copies:
        copy.wait()
    scale = 1.0 / math.sqrt(HD) * math.log2(math.e)
    share = tiles // pairs
    for start in range(0, tiles, GROUP):
        block = (first_ref[1] + start // share) % pairs * share
        group = [block + (start + g) % share for g in range(GROUP)]
        blocks = [
            [own_ref.at[i]] + [held.at[source_ref[j, first_ref[0] + i]] for j in range(1, KT)] for i in group
        ]
        work = [(g, h) for g in range(GROUP) for h in range(heads)]
        scores = [
            [
                lax.dot_general(
                    queries_ref[group[g], :, h * HD : (h + 1) * HD],
                    b[:, h * HD : (h + 1) * HD],
                    (((1,), (1,)), ((), ())),
                    preferred_element_type=jnp.float32,
                )
                for b in blocks[g]
            ]
            for g, h in work
        ]
        highest = [jnp.max(functools.reduce(jnp.maximum, s), axis=-1, keepdims=True) * scale for s in scores]
        exponents = [[jnp.exp2(x * scale - m) for x in s] for s, m in zip(scores, highest)]
        totals = [jnp.sum(functools.reduce(jnp.add, e), axis=-1, keepdims=True) for e in exponents]
        for (g, h), e, total in zip(work, exponents, totals):
            weights = jnp.concatenate([x.astype(jnp.bfloat16) for x in e], axis=1)
            upper = slice((heads + h) * HD, (heads + h + 1) * HD)
            values = jnp.concatenate([b[:, upper] for b in blocks[g]], axis=0)
            attended = jnp.dot(weights, values, preferred_element_type=jnp.float32)
            row = (start + g) % share * TILE
            out_refs[start // share][row : row + TILE, h * HD : (h + 1) * HD] = (
                attended * (1.0 / total)
            ).astype(jnp.bfloat16)


def attend(first, source, queries, own, incoming, pairs):
    tiles = own.shape[0]
    vmem, smem = pl.BlockSpec(memory_space=pltpu.VMEM), pl.BlockSpec(memory_space=pltpu.SMEM)
    return pl.pallas_call(
        functools.partial(attend_kernel, tiles=tiles, heads=queries.shape[2] // HD, pairs=pairs),
        in_specs=[smem, smem, vmem, vmem] + [pl.BlockSpec(memory_space=pl.ANY)] * len(incoming),
        out_specs=[vmem] * pairs,
        out_shape=[jax.ShapeDtypeStruct((tiles * TILE // pairs, queries.shape[2]), jnp.bfloat16)] * pairs,
        scratch_shapes=[
            pltpu.VMEM((SIDE * SIDE * CAP,) + own.shape[1:], jnp.bfloat16),
            pltpu.SemaphoreType.DMA((len(incoming),)),
        ],
        compiler_params=pltpu.CompilerParams(vmem_limit_bytes=VMEM),
        name="attend",
    )(first, source, queries, own, *incoming)


def mix_kernel(half_ref, *refs):
    out_ref, count = refs[-1], len(refs) // 2
    parts = [
        jnp.dot(left[0], right[...], preferred_element_type=jnp.float32)
        for left, right in zip(refs[:count], refs[count:])
    ]
    out_ref[...] = functools.reduce(jnp.add, parts).astype(out_ref.dtype)


def mix(half, attended, weights, dtype):
    rows, width = attended[0].shape
    model = weights[0].shape[1]
    return pl.pallas_call(
        mix_kernel,
        grid_spec=pltpu.PrefetchScalarGridSpec(
            num_scalar_prefetch=1,
            grid=(model // COLUMNS,),
            in_specs=[pl.BlockSpec((1, rows // 2, width), lambda i, h: (h[0], 0, 0))] * len(attended)
            + [pl.BlockSpec((width, COLUMNS), lambda i, h: (0, i))] * len(weights),
            out_specs=pl.BlockSpec((rows // 2, COLUMNS), lambda i, h: (0, i)),
        ),
        out_shape=jax.ShapeDtypeStruct((rows // 2, model), dtype),
        compiler_params=pltpu.CompilerParams(vmem_limit_bytes=LEAST),
        name="mix",
    )(half, *[x.reshape(2, rows // 2, width) for x in attended], *weights)


def body(tokens, norm_gain, in_weight, out_weight, pattern):
    shards = lax.axis_size("seq")
    groups = lax.axis_size("head")
    myself = lax.axis_index("seq")
    row_count, model = tokens.shape
    tiles = row_count // TILE
    width = in_weight.shape[2]
    heads = width // HD
    me = jnp.reshape(myself, (1,)).astype(jnp.int32)

    pairs = groups // 2
    place = lax.axis_index("head")
    pair, core = place // 2, place % 2

    def along(x, shift):
        return lax.ppermute(x, "head", [(s, (s // 2 + shift) % pairs * 2 + s % 2) for s in range(groups)])

    chosen, source = pl.pallas_call(
        functools.partial(tables_kernel, shards=shards, tiles=tiles),
        in_specs=[pl.BlockSpec(memory_space=pltpu.SMEM), pl.BlockSpec(memory_space=pltpu.VMEM)],
        out_shape=[
            jax.ShapeDtypeStruct((8, 128), jnp.int32),
            jax.ShapeDtypeStruct((KT, shards * tiles), jnp.int32),
        ],
        name="tables",
    )(me, pattern.T)

    gain = norm_gain.reshape(model // HD, HD)
    weights = in_weight.transpose(1, 0, 2)
    mixers = {shift: along(out_weight, shift) for shift in (1, 3)}
    own, queries = project(
        tokens, gain, weights, [(1, 0, heads), (2, 0, heads), (0, 0, heads)], [2 * width, width], MOST
    )
    sends = dispatch(me, chosen, own, SHIFTS)
    sends, mixers = lax.optimization_barrier((sends, mixers))
    incoming = []
    for p, shift in enumerate(SHIFTS):
        send = sends[p]
        incoming.append(lax.ppermute(send, "seq", [(s, shifted(s, shift)) for s in range(shards)]))
    late, incoming[LATE] = lax.optimization_barrier((out_weight, incoming[LATE]))
    mixers[2] = along(late, 2)
    first = jnp.stack([myself * tiles, pair]).astype(jnp.int32)
    attended = attend(first, source, queries, own, incoming, pairs)
    lefts = [attended[0]] + [along(attended[shift], shift) for shift in range(1, pairs)]
    rights = [out_weight] + [mixers[shift] for shift in range(1, pairs)]
    give = mix(jnp.reshape(1 - core, (1,)).astype(jnp.int32), lefts, rights, jnp.bfloat16)
    got = lax.ppermute(give, "head", [(s, s + 1 - s % 2 * 2) for s in range(groups)])
    keep = mix(jnp.reshape(core, (1,)).astype(jnp.int32), lefts, rights, jnp.float32)
    return (keep + got.astype(jnp.float32)).astype(jnp.bfloat16)


def solution(mesh):
    return jax.shard_map(
        body,
        mesh=mesh,
        in_specs=(P("seq", None), P(), P(None, None, "head"), P("head", None), P()),
        out_specs=P(("seq", "head"), None),
        check_vma=False,
    )
```

```python
import functools
import math

import jax
import jax.numpy as jnp
from jax import lax
from jax.experimental import pallas as pl
from jax.experimental.pallas import tpu as pltpu
from jax.sharding import PartitionSpec as P

HD = 128
TILE = 128
KT = 4
CAP = 4
BLOCK = 512
GROUP = 2
SIDE = 4
SHIFTS = (10, 6, 12, 14, 4, 3, 11, 1, 5, 15, 9, 7, 13, 2, 8)
FIRST = 5
ALONE = 2
LATE = 10
COLUMNS = 1024
VMEM = 60 * 1024 * 1024
MOST = 60 * 1024 * 1024
LEAST = 16 * 1024 * 1024


def shift_of(source, target):
    rows = (target // SIDE - source // SIDE + SIDE) % SIDE
    return rows * SIDE + (target % SIDE - source % SIDE + SIDE) % SIDE


def shifted(source, shift):
    return (source // SIDE + shift // SIDE) % SIDE * SIDE + (source % SIDE + shift % SIDE) % SIDE


def tables_kernel(me_ref, pattern_ref, chosen_ref, source_ref, *, shards, tiles):
    total = shards * tiles
    table = pattern_ref[...]
    owner = table // tiles
    local = table % tiles
    row = lax.broadcasted_iota(jnp.int32, (total, total), 0)
    col = lax.broadcasted_iota(jnp.int32, (total, total), 1)
    same = (row // tiles) == (col // tiles)
    every = same.astype(jnp.bfloat16)
    before = (same & (row < col)).astype(jnp.bfloat16)
    index = lax.broadcasted_iota(jnp.int32, (shards, total), 0)
    names = [(owner[c : c + 1] == index).astype(jnp.bfloat16) for c in range(1, KT)]
    dot = functools.partial(jnp.dot, preferred_element_type=jnp.float32)
    earlier = jnp.zeros((shards, total), jnp.float32)
    picked = [jnp.zeros((1, total), jnp.float32) for _ in range(CAP)]
    source_ref[0:1, :] = jnp.zeros((1, total), jnp.int32)
    for c in range(1, KT):
        here = names[c - 1]
        rank = jnp.sum(here.astype(jnp.float32) * (dot(here, before) + earlier), axis=0, keepdims=True)
        earlier = earlier + dot(here, every)
        rank = rank.astype(jnp.int32)
        mine = owner[c : c + 1] == me_ref[0]
        source_ref[c : c + 1, :] = shift_of(owner[c : c + 1], me_ref[0]) * CAP + rank
        for k in range(CAP):
            picked[k] += jnp.where(mine & (rank == k), local[c : c + 1], 0).astype(jnp.float32)
    tile_row = lax.broadcasted_iota(jnp.int32, (total, 128), 0)
    lane = lax.broadcasted_iota(jnp.int32, (total, 128), 1)
    spread = ((tile_row // tiles) == lane).astype(jnp.bfloat16)
    for k in range(CAP):
        chosen_ref[k : k + 1, :] = dot(picked[k].astype(jnp.bfloat16), spread).astype(jnp.int32)


def project_kernel(*refs, widths, scales):
    count = len(widths)
    tokens_ref, gain_ref = refs[0], refs[1]
    weight_refs = refs[2 : 2 + count]
    out_refs = refs[2 + count : 2 + count + scales]
    scaled_ref = refs[-1]
    model = scaled_ref.shape[0]
    step = pl.program_id(0)

    @pl.when(step == 0)
    def _():
        gains = jnp.transpose(gain_ref[...])
        for j in range(model // HD):
            rows = slice(j * HD, (j + 1) * HD)
            at = 0
            for ref, width in zip(weight_refs, widths):
                part = ref[0, rows, :].astype(jnp.float32) * gains[:, j : j + 1]
                scaled_ref[rows, at : at + width] = part.astype(jnp.bfloat16)
                at += width

    tokens = tokens_ref[...]
    values = tokens.astype(jnp.float32)
    inverse = lax.rsqrt(jnp.mean(values * values, axis=-1, keepdims=True) + 1e-05)
    result = jnp.dot(tokens, scaled_ref[...], preferred_element_type=jnp.float32) * inverse
    result = result.astype(jnp.bfloat16)
    at = 0
    for ref in out_refs:
        width = ref.shape[2]
        ref[...] = result[:, at : at + width].reshape(ref.shape)
        at += width


def project(tokens, gain, weights, columns, outs, limit):
    rows, model = tokens.shape
    tiles, count = rows // TILE, BLOCK // TILE
    widths = [n * HD for _, _, n in columns]
    return pl.pallas_call(
        functools.partial(project_kernel, widths=widths, scales=len(outs)),
        grid=(rows // BLOCK,),
        in_specs=[
            pl.BlockSpec((BLOCK, model), lambda i: (i, 0)),
            pl.BlockSpec(gain.shape, lambda i: (0, 0)),
        ]
        + [
            pl.BlockSpec((1, model, n * HD), lambda i, c=c, b=b: (c, 0, b), pipeline_mode=pl.Buffered(1))
            for c, b, n in columns
        ],
        out_specs=[pl.BlockSpec((count, TILE, width), lambda i: (i, 0, 0)) for width in outs],
        out_shape=[jax.ShapeDtypeStruct((tiles, TILE, width), jnp.bfloat16) for width in outs],
        scratch_shapes=[pltpu.VMEM((model, sum(widths)), jnp.bfloat16)],
        compiler_params=pltpu.CompilerParams(vmem_limit_bytes=limit),
        name="project",
    )(tokens, gain, *([weights] * len(columns)))


def dispatch_kernel(me_ref, chosen_ref, held_ref, *rest, shifts):
    send_refs, staged, semaphores = rest[:-2], rest[-2], rest[-1]
    copies = []
    for p, shift in enumerate(shifts):
        target = shifted(me_ref[0], shift)
        for k in range(CAP):
            staged[p, k] = held_ref[chosen_ref[k, target]]
        copies.append(pltpu.make_async_copy(staged.at[p], send_refs[p], semaphores.at[p]))
        copies[-1].start()
    for copy in copies:
        copy.wait()


def dispatch(me, chosen, held, shifts):
    shape = (CAP,) + held.shape[1:]
    smem = pl.BlockSpec(memory_space=pltpu.SMEM)
    return pl.pallas_call(
        functools.partial(dispatch_kernel, shifts=shifts),
        in_specs=[smem, smem, pl.BlockSpec(memory_space=pltpu.VMEM)],
        out_specs=[pl.BlockSpec(memory_space=pltpu.HBM)] * len(shifts),
        out_shape=[jax.ShapeDtypeStruct(shape, held.dtype)] * len(shifts),
        scratch_shapes=[
            pltpu.VMEM((len(shifts),) + shape, held.dtype),
            pltpu.SemaphoreType.DMA((len(shifts),)),
        ],
        compiler_params=pltpu.CompilerParams(vmem_limit_bytes=MOST),
        name="dispatch",
    )(me, chosen, held)


def attend_kernel(first_ref, source_ref, queries_ref, own_ref, *rest, tiles, heads, pairs):
    incoming_refs, out_refs, held, semaphores = rest[: -2 - pairs], rest[-2 - pairs : -2], rest[-2], rest[-1]
    copies = []
    for p, shift in enumerate(SHIFTS):
        copies.append(
            pltpu.make_async_copy(incoming_refs[p], held.at[pl.ds(shift * CAP, CAP)], semaphores.at[p])
        )
        copies[-1].start()
    for copy in copies:
        copy.wait()
    scale = 1.0 / math.sqrt(HD) * math.log2(math.e)
    share = tiles // pairs
    for start in range(0, tiles, GROUP):
        block = (first_ref[1] + start // share) % pairs * share
        group = [block + (start + g) % share for g in range(GROUP)]
        blocks = [
            [own_ref.at[i]] + [held.at[source_ref[j, first_ref[0] + i]] for j in range(1, KT)] for i in group
        ]
        work = [(g, h) for g in range(GROUP) for h in range(heads)]
        scores = [
            [
                lax.dot_general(
                    queries_ref[group[g], :, h * HD : (h + 1) * HD],
                    b[:, h * HD : (h + 1) * HD],
                    (((1,), (1,)), ((), ())),
                    preferred_element_type=jnp.float32,
                )
                for b in blocks[g]
            ]
            for g, h in work
        ]
        highest = [jnp.max(functools.reduce(jnp.maximum, s), axis=-1, keepdims=True) * scale for s in scores]
        exponents = [[jnp.exp2(x * scale - m) for x in s] for s, m in zip(scores, highest)]
        totals = [jnp.sum(functools.reduce(jnp.add, e), axis=-1, keepdims=True) for e in exponents]
        for (g, h), e, total in zip(work, exponents, totals):
            weights = jnp.concatenate([x.astype(jnp.bfloat16) for x in e], axis=1)
            upper = slice((heads + h) * HD, (heads + h + 1) * HD)
            values = jnp.concatenate([b[:, upper] for b in blocks[g]], axis=0)
            attended = jnp.dot(weights, values, preferred_element_type=jnp.float32)
            row = (start + g) % share * TILE
            out_refs[start // share][row : row + TILE, h * HD : (h + 1) * HD] = (
                attended * (1.0 / total)
            ).astype(jnp.bfloat16)


def attend(first, source, queries, own, incoming, pairs):
    tiles = own.shape[0]
    vmem, smem = pl.BlockSpec(memory_space=pltpu.VMEM), pl.BlockSpec(memory_space=pltpu.SMEM)
    return pl.pallas_call(
        functools.partial(attend_kernel, tiles=tiles, heads=queries.shape[2] // HD, pairs=pairs),
        in_specs=[smem, smem, vmem, vmem] + [pl.BlockSpec(memory_space=pl.ANY)] * len(incoming),
        out_specs=[vmem] * pairs,
        out_shape=[jax.ShapeDtypeStruct((tiles * TILE // pairs, queries.shape[2]), jnp.bfloat16)] * pairs,
        scratch_shapes=[
            pltpu.VMEM((SIDE * SIDE * CAP,) + own.shape[1:], jnp.bfloat16),
            pltpu.SemaphoreType.DMA((len(incoming),)),
        ],
        compiler_params=pltpu.CompilerParams(vmem_limit_bytes=VMEM),
        name="attend",
    )(first, source, queries, own, *incoming)


def mix_kernel(half_ref, *refs):
    out_ref, count = refs[-1], len(refs) // 2
    parts = [
        jnp.dot(left[0], right[...], preferred_element_type=jnp.float32)
        for left, right in zip(refs[:count], refs[count:])
    ]
    out_ref[...] = functools.reduce(jnp.add, parts).astype(out_ref.dtype)


def mix(half, attended, weights, dtype):
    rows, width = attended[0].shape
    model = weights[0].shape[1]
    return pl.pallas_call(
        mix_kernel,
        grid_spec=pltpu.PrefetchScalarGridSpec(
            num_scalar_prefetch=1,
            grid=(model // COLUMNS,),
            in_specs=[pl.BlockSpec((1, rows // 2, width), lambda i, h: (h[0], 0, 0))] * len(attended)
            + [pl.BlockSpec((width, COLUMNS), lambda i, h: (0, i))] * len(weights),
            out_specs=pl.BlockSpec((rows // 2, COLUMNS), lambda i, h: (0, i)),
        ),
        out_shape=jax.ShapeDtypeStruct((rows // 2, model), dtype),
        compiler_params=pltpu.CompilerParams(vmem_limit_bytes=LEAST),
        name="mix",
    )(half, *[x.reshape(2, rows // 2, width) for x in attended], *weights)


def body(tokens, norm_gain, in_weight, out_weight, pattern):
    shards = lax.axis_size("seq")
    groups = lax.axis_size("head")
    myself = lax.axis_index("seq")
    row_count, model = tokens.shape
    tiles = row_count // TILE
    width = in_weight.shape[2]
    heads = width // HD
    me = jnp.reshape(myself, (1,)).astype(jnp.int32)

    pairs = groups // 2
    place = lax.axis_index("head")
    pair, core = place // 2, place % 2

    def along(x, shift):
        return lax.ppermute(x, "head", [(s, (s // 2 + shift) % pairs * 2 + s % 2) for s in range(groups)])

    chosen, source = pl.pallas_call(
        functools.partial(tables_kernel, shards=shards, tiles=tiles),
        in_specs=[pl.BlockSpec(memory_space=pltpu.SMEM), pl.BlockSpec(memory_space=pltpu.VMEM)],
        out_shape=[
            jax.ShapeDtypeStruct((8, 128), jnp.int32),
            jax.ShapeDtypeStruct((KT, shards * tiles), jnp.int32),
        ],
        name="tables",
    )(me, pattern.T)

    gain = norm_gain.reshape(model // HD, HD)
    weights = in_weight.transpose(1, 0, 2)
    mixers = {shift: along(out_weight, shift) for shift in (1, 3)}
    (own,) = project(tokens, gain, weights, [(1, 0, heads), (2, 0, heads)], [2 * width], MOST)
    sends = list(dispatch(me, chosen, own, SHIFTS[:FIRST]))
    held, tokens, sends = lax.optimization_barrier((own, tokens, sends))
    sends += list(dispatch(me, chosen, held, SHIFTS[FIRST:]))
    (queries,) = project(tokens, gain, weights, [(0, 0, heads)], [width], MOST)
    sends[ALONE:], mixers = lax.optimization_barrier((sends[ALONE:], mixers))
    incoming = []
    for p, shift in enumerate(SHIFTS):
        send = sends[p]
        incoming.append(lax.ppermute(send, "seq", [(s, shifted(s, shift)) for s in range(shards)]))
    late, incoming[LATE] = lax.optimization_barrier((out_weight, incoming[LATE]))
    mixers[2] = along(late, 2)
    first = jnp.stack([myself * tiles, pair]).astype(jnp.int32)
    attended = attend(first, source, queries, own, incoming, pairs)
    lefts = [attended[0]] + [along(attended[shift], shift) for shift in range(1, pairs)]
    rights = [out_weight] + [mixers[shift] for shift in range(1, pairs)]
    give = mix(jnp.reshape(1 - core, (1,)).astype(jnp.int32), lefts, rights, jnp.bfloat16)
    got = lax.ppermute(give, "head", [(s, s + 1 - s % 2 * 2) for s in range(groups)])
    keep = mix(jnp.reshape(core, (1,)).astype(jnp.int32), lefts, rights, jnp.float32)
    return (keep + got.astype(jnp.float32)).astype(jnp.bfloat16)


def solution(mesh):
    return jax.shard_map(
        body,
        mesh=mesh,
        in_specs=(P("seq", None), P(), P(None, None, "head"), P("head", None), P()),
        out_specs=P(("seq", "head"), None),
        check_vma=False,
    )
```

```python
import functools
import math

import jax
import jax.numpy as jnp
from jax import lax
from jax.experimental import pallas as pl
from jax.experimental.pallas import tpu as pltpu
from jax.sharding import PartitionSpec as P

HD = 128
TILE = 128
KT = 4
CAP = 4
BLOCK = 512
GROUP = 2
SIDE = 4
SHIFTS = (10, 6, 12, 14, 4, 3, 11, 1, 5, 15, 9, 7, 13, 2, 8)
FIRST = 5
STEPS = ((1, 2, 3), (0,))
ALONE = 2
LATE = 10
COLUMNS = 1024
VMEM = 60 * 1024 * 1024
MOST = 60 * 1024 * 1024
LEAST = 16 * 1024 * 1024


def shift_of(source, target):
    rows = (target // SIDE - source // SIDE + SIDE) % SIDE
    return rows * SIDE + (target % SIDE - source % SIDE + SIDE) % SIDE


def shifted(source, shift):
    return (source // SIDE + shift // SIDE) % SIDE * SIDE + (source % SIDE + shift % SIDE) % SIDE


def tables_kernel(me_ref, pattern_ref, chosen_ref, source_ref, *, shards, tiles):
    total = shards * tiles
    table = pattern_ref[...]
    owner = table // tiles
    local = table % tiles
    row = lax.broadcasted_iota(jnp.int32, (total, total), 0)
    col = lax.broadcasted_iota(jnp.int32, (total, total), 1)
    same = (row // tiles) == (col // tiles)
    every = same.astype(jnp.bfloat16)
    before = (same & (row < col)).astype(jnp.bfloat16)
    index = lax.broadcasted_iota(jnp.int32, (shards, total), 0)
    names = [(owner[c : c + 1] == index).astype(jnp.bfloat16) for c in range(1, KT)]
    dot = functools.partial(jnp.dot, preferred_element_type=jnp.float32)
    earlier = jnp.zeros((shards, total), jnp.float32)
    picked = [jnp.zeros((1, total), jnp.float32) for _ in range(CAP)]
    source_ref[0:1, :] = jnp.zeros((1, total), jnp.int32)
    for c in range(1, KT):
        here = names[c - 1]
        rank = jnp.sum(here.astype(jnp.float32) * (dot(here, before) + earlier), axis=0, keepdims=True)
        earlier = earlier + dot(here, every)
        rank = rank.astype(jnp.int32)
        mine = owner[c : c + 1] == me_ref[0]
        source_ref[c : c + 1, :] = shift_of(owner[c : c + 1], me_ref[0]) * CAP + rank
        for k in range(CAP):
            picked[k] += jnp.where(mine & (rank == k), local[c : c + 1], 0).astype(jnp.float32)
    tile_row = lax.broadcasted_iota(jnp.int32, (total, 128), 0)
    lane = lax.broadcasted_iota(jnp.int32, (total, 128), 1)
    spread = ((tile_row // tiles) == lane).astype(jnp.bfloat16)
    for k in range(CAP):
        chosen_ref[k : k + 1, :] = dot(picked[k].astype(jnp.bfloat16), spread).astype(jnp.int32)


def project_kernel(*refs, widths, scales):
    count = len(widths)
    tokens_ref, gain_ref = refs[0], refs[1]
    weight_refs = refs[2 : 2 + count]
    out_refs = refs[2 + count : 2 + count + scales]
    scaled_ref = refs[-1]
    model = scaled_ref.shape[0]
    step = pl.program_id(0)

    @pl.when(step == 0)
    def _():
        gains = jnp.transpose(gain_ref[...])
        for j in range(model // HD):
            rows = slice(j * HD, (j + 1) * HD)
            at = 0
            for ref, width in zip(weight_refs, widths):
                part = ref[0, rows, :].astype(jnp.float32) * gains[:, j : j + 1]
                scaled_ref[rows, at : at + width] = part.astype(jnp.bfloat16)
                at += width

    tokens = tokens_ref[...]
    values = tokens.astype(jnp.float32)
    inverse = lax.rsqrt(jnp.mean(values * values, axis=-1, keepdims=True) + 1e-05)
    result = jnp.dot(tokens, scaled_ref[...], preferred_element_type=jnp.float32) * inverse
    result = result.astype(jnp.bfloat16)
    at = 0
    for ref in out_refs:
        width = ref.shape[2]
        ref[...] = result[:, at : at + width].reshape(ref.shape)
        at += width


def project(tokens, gain, weights, columns, outs, limit):
    rows, model = tokens.shape
    tiles, count = rows // TILE, BLOCK // TILE
    widths = [n * HD for _, _, n in columns]
    return pl.pallas_call(
        functools.partial(project_kernel, widths=widths, scales=len(outs)),
        grid=(rows // BLOCK,),
        in_specs=[
            pl.BlockSpec((BLOCK, model), lambda i: (i, 0)),
            pl.BlockSpec(gain.shape, lambda i: (0, 0)),
        ]
        + [
            pl.BlockSpec((1, model, n * HD), lambda i, c=c, b=b: (c, 0, b), pipeline_mode=pl.Buffered(1))
            for c, b, n in columns
        ],
        out_specs=[pl.BlockSpec((count, TILE, width), lambda i: (i, 0, 0)) for width in outs],
        out_shape=[jax.ShapeDtypeStruct((tiles, TILE, width), jnp.bfloat16) for width in outs],
        scratch_shapes=[pltpu.VMEM((model, sum(widths)), jnp.bfloat16)],
        compiler_params=pltpu.CompilerParams(vmem_limit_bytes=limit),
        name="project",
    )(tokens, gain, *([weights] * len(columns)))


def dispatch_kernel(me_ref, chosen_ref, held_ref, *rest, shifts):
    send_refs, staged, semaphores = rest[:-2], rest[-2], rest[-1]
    copies = []
    for p, shift in enumerate(shifts):
        target = shifted(me_ref[0], shift)
        for k in range(CAP):
            staged[p, k] = held_ref[chosen_ref[k, target]]
        copies.append(pltpu.make_async_copy(staged.at[p], send_refs[p], semaphores.at[p]))
        copies[-1].start()
    for copy in copies:
        copy.wait()


def dispatch(me, chosen, held, shifts):
    shape = (CAP,) + held.shape[1:]
    smem = pl.BlockSpec(memory_space=pltpu.SMEM)
    return pl.pallas_call(
        functools.partial(dispatch_kernel, shifts=shifts),
        in_specs=[smem, smem, pl.BlockSpec(memory_space=pltpu.VMEM)],
        out_specs=[pl.BlockSpec(memory_space=pltpu.HBM)] * len(shifts),
        out_shape=[jax.ShapeDtypeStruct(shape, held.dtype)] * len(shifts),
        scratch_shapes=[
            pltpu.VMEM((len(shifts),) + shape, held.dtype),
            pltpu.SemaphoreType.DMA((len(shifts),)),
        ],
        compiler_params=pltpu.CompilerParams(vmem_limit_bytes=MOST),
        name="dispatch",
    )(me, chosen, held)


def attend_kernel(first_ref, source_ref, queries_ref, own_ref, *rest, tiles, heads, pairs, steps):
    count = len(steps)
    incoming_refs, out_refs, held, semaphores = rest[: -2 - count], rest[-2 - count : -2], rest[-2], rest[-1]
    copies = []
    for p, shift in enumerate(SHIFTS):
        copies.append(
            pltpu.make_async_copy(incoming_refs[p], held.at[pl.ds(shift * CAP, CAP)], semaphores.at[p])
        )
        copies[-1].start()
    for copy in copies:
        copy.wait()
    scale = 1.0 / math.sqrt(HD) * math.log2(math.e)
    share = tiles // pairs
    for start in range(0, share * count, GROUP):
        block = (first_ref[1] + steps[start // share]) % pairs * share
        group = [block + (start + g) % share for g in range(GROUP)]
        blocks = [
            [own_ref.at[i]] + [held.at[source_ref[j, first_ref[0] + i]] for j in range(1, KT)] for i in group
        ]
        work = [(g, h) for g in range(GROUP) for h in range(heads)]
        scores = [
            [
                lax.dot_general(
                    queries_ref[group[g], :, h * HD : (h + 1) * HD],
                    b[:, h * HD : (h + 1) * HD],
                    (((1,), (1,)), ((), ())),
                    preferred_element_type=jnp.float32,
                )
                for b in blocks[g]
            ]
            for g, h in work
        ]
        highest = [jnp.max(functools.reduce(jnp.maximum, s), axis=-1, keepdims=True) * scale for s in scores]
        exponents = [[jnp.exp2(x * scale - m) for x in s] for s, m in zip(scores, highest)]
        totals = [jnp.sum(functools.reduce(jnp.add, e), axis=-1, keepdims=True) for e in exponents]
        for (g, h), e, total in zip(work, exponents, totals):
            weights = jnp.concatenate([x.astype(jnp.bfloat16) for x in e], axis=1)
            upper = slice((heads + h) * HD, (heads + h + 1) * HD)
            values = jnp.concatenate([b[:, upper] for b in blocks[g]], axis=0)
            attended = jnp.dot(weights, values, preferred_element_type=jnp.float32)
            row = (start + g) % share * TILE
            out_refs[start // share][row : row + TILE, h * HD : (h + 1) * HD] = (
                attended * (1.0 / total)
            ).astype(jnp.bfloat16)


def attend(first, source, queries, own, incoming, pairs, steps):
    tiles = own.shape[0]
    vmem, smem = pl.BlockSpec(memory_space=pltpu.VMEM), pl.BlockSpec(memory_space=pltpu.SMEM)
    return pl.pallas_call(
        functools.partial(attend_kernel, tiles=tiles, heads=queries.shape[2] // HD, pairs=pairs, steps=steps),
        in_specs=[smem, smem, vmem, vmem] + [pl.BlockSpec(memory_space=pl.ANY)] * len(incoming),
        out_specs=[vmem] * len(steps),
        out_shape=[jax.ShapeDtypeStruct((tiles * TILE // pairs, queries.shape[2]), jnp.bfloat16)] * len(steps),
        scratch_shapes=[
            pltpu.VMEM((SIDE * SIDE * CAP,) + own.shape[1:], jnp.bfloat16),
            pltpu.SemaphoreType.DMA((len(incoming),)),
        ],
        compiler_params=pltpu.CompilerParams(vmem_limit_bytes=VMEM),
        name="attend",
    )(first, source, queries, own, *incoming)


def mix_kernel(half_ref, *refs):
    out_ref, count = refs[-1], len(refs) // 2
    parts = [
        jnp.dot(left[0], right[...], preferred_element_type=jnp.float32)
        for left, right in zip(refs[:count], refs[count:])
    ]
    out_ref[...] = functools.reduce(jnp.add, parts).astype(out_ref.dtype)


def mix(half, attended, weights, dtype):
    rows, width = attended[0].shape
    model = weights[0].shape[1]
    return pl.pallas_call(
        mix_kernel,
        grid_spec=pltpu.PrefetchScalarGridSpec(
            num_scalar_prefetch=1,
            grid=(model // COLUMNS,),
            in_specs=[pl.BlockSpec((1, rows // 2, width), lambda i, h: (h[0], 0, 0))] * len(attended)
            + [pl.BlockSpec((width, COLUMNS), lambda i, h: (0, i))] * len(weights),
            out_specs=pl.BlockSpec((rows // 2, COLUMNS), lambda i, h: (0, i)),
        ),
        out_shape=jax.ShapeDtypeStruct((rows // 2, model), dtype),
        compiler_params=pltpu.CompilerParams(vmem_limit_bytes=LEAST),
        name="mix",
    )(half, *[x.reshape(2, rows // 2, width) for x in attended], *weights)


def body(tokens, norm_gain, in_weight, out_weight, pattern):
    shards = lax.axis_size("seq")
    groups = lax.axis_size("head")
    myself = lax.axis_index("seq")
    row_count, model = tokens.shape
    tiles = row_count // TILE
    width = in_weight.shape[2]
    heads = width // HD
    me = jnp.reshape(myself, (1,)).astype(jnp.int32)

    pairs = groups // 2
    place = lax.axis_index("head")
    pair, core = place // 2, place % 2

    def along(x, shift):
        return lax.ppermute(x, "head", [(s, (s // 2 + shift) % pairs * 2 + s % 2) for s in range(groups)])

    chosen, source = pl.pallas_call(
        functools.partial(tables_kernel, shards=shards, tiles=tiles),
        in_specs=[pl.BlockSpec(memory_space=pltpu.SMEM), pl.BlockSpec(memory_space=pltpu.VMEM)],
        out_shape=[
            jax.ShapeDtypeStruct((8, 128), jnp.int32),
            jax.ShapeDtypeStruct((KT, shards * tiles), jnp.int32),
        ],
        name="tables",
    )(me, pattern.T)

    gain = norm_gain.reshape(model // HD, HD)
    weights = in_weight.transpose(1, 0, 2)
    mixers = {shift: along(out_weight, shift) for shift in (1, 3)}
    (own,) = project(tokens, gain, weights, [(1, 0, heads), (2, 0, heads)], [2 * width], MOST)
    sends = list(dispatch(me, chosen, own, SHIFTS[:FIRST]))
    held, tokens, sends = lax.optimization_barrier((own, tokens, sends))
    sends += list(dispatch(me, chosen, held, SHIFTS[FIRST:]))
    (queries,) = project(tokens, gain, weights, [(0, 0, heads)], [width], MOST)
    sends[ALONE:], mixers = lax.optimization_barrier((sends[ALONE:], mixers))
    incoming = []
    for p, shift in enumerate(SHIFTS):
        send = sends[p]
        incoming.append(lax.ppermute(send, "seq", [(s, shifted(s, shift)) for s in range(shards)]))
    late, incoming[LATE] = lax.optimization_barrier((out_weight, incoming[LATE]))
    mixers[2] = along(late, 2)
    first = jnp.stack([myself * tiles, pair]).astype(jnp.int32)
    lefts = {}
    for steps in STEPS:
        for step, block in zip(steps, attend(first, source, queries, own, incoming, pairs, steps)):
            lefts[step] = along(block, step) if step else block
    lefts = [lefts[step] for step in range(pairs)]
    rights = [out_weight] + [mixers[shift] for shift in range(1, pairs)]
    give = mix(jnp.reshape(1 - core, (1,)).astype(jnp.int32), lefts, rights, jnp.bfloat16)
    got = lax.ppermute(give, "head", [(s, s + 1 - s % 2 * 2) for s in range(groups)])
    keep = mix(jnp.reshape(core, (1,)).astype(jnp.int32), lefts, rights, jnp.float32)
    return (keep + got.astype(jnp.float32)).astype(jnp.bfloat16)


def solution(mesh):
    return jax.shard_map(
        body,
        mesh=mesh,
        in_specs=(P("seq", None), P(), P(None, None, "head"), P("head", None), P()),
        out_specs=P(("seq", "head"), None),
        check_vma=False,
    )
```

```python
import functools
import math

import jax
import jax.numpy as jnp
from jax import lax
from jax.experimental import pallas as pl
from jax.experimental.pallas import tpu as pltpu
from jax.sharding import PartitionSpec as P

HD = 128
TILE = 128
KT = 4
CAP = 4
BLOCK = 512
GROUP = 2
SIDE = 4
SHIFTS = (10, 6, 12, 14, 4, 3, 11, 1, 5, 15, 9, 7, 13, 2, 8)
FIRST = 2
STEPS = ((1, 2, 3), (0,))
ALONE = 2
LATE = 10
COLUMNS = 1024
VMEM = 60 * 1024 * 1024
MOST = 60 * 1024 * 1024
LEAST = 16 * 1024 * 1024


def shift_of(source, target):
    rows = (target // SIDE - source // SIDE + SIDE) % SIDE
    return rows * SIDE + (target % SIDE - source % SIDE + SIDE) % SIDE


def shifted(source, shift):
    return (source // SIDE + shift // SIDE) % SIDE * SIDE + (source % SIDE + shift % SIDE) % SIDE


def tables_kernel(me_ref, pattern_ref, chosen_ref, source_ref, *, shards, tiles):
    total = shards * tiles
    table = pattern_ref[...]
    owner = table // tiles
    local = table % tiles
    row = lax.broadcasted_iota(jnp.int32, (total, total), 0)
    col = lax.broadcasted_iota(jnp.int32, (total, total), 1)
    same = (row // tiles) == (col // tiles)
    every = same.astype(jnp.bfloat16)
    before = (same & (row < col)).astype(jnp.bfloat16)
    index = lax.broadcasted_iota(jnp.int32, (shards, total), 0)
    names = [(owner[c : c + 1] == index).astype(jnp.bfloat16) for c in range(1, KT)]
    dot = functools.partial(jnp.dot, preferred_element_type=jnp.float32)
    earlier = jnp.zeros((shards, total), jnp.float32)
    picked = [jnp.zeros((1, total), jnp.float32) for _ in range(CAP)]
    source_ref[0:1, :] = jnp.zeros((1, total), jnp.int32)
    for c in range(1, KT):
        here = names[c - 1]
        rank = jnp.sum(here.astype(jnp.float32) * (dot(here, before) + earlier), axis=0, keepdims=True)
        earlier = earlier + dot(here, every)
        rank = rank.astype(jnp.int32)
        mine = owner[c : c + 1] == me_ref[0]
        source_ref[c : c + 1, :] = shift_of(owner[c : c + 1], me_ref[0]) * CAP + rank
        for k in range(CAP):
            picked[k] += jnp.where(mine & (rank == k), local[c : c + 1], 0).astype(jnp.float32)
    tile_row = lax.broadcasted_iota(jnp.int32, (total, 128), 0)
    lane = lax.broadcasted_iota(jnp.int32, (total, 128), 1)
    spread = ((tile_row // tiles) == lane).astype(jnp.bfloat16)
    for k in range(CAP):
        chosen_ref[k : k + 1, :] = dot(picked[k].astype(jnp.bfloat16), spread).astype(jnp.int32)


def project_kernel(*refs, widths, scales):
    count = len(widths)
    tokens_ref, gain_ref = refs[0], refs[1]
    weight_refs = refs[2 : 2 + count]
    out_refs = refs[2 + count : 2 + count + scales]
    scaled_ref = refs[-1]
    model = scaled_ref.shape[0]
    step = pl.program_id(0)

    @pl.when(step == 0)
    def _():
        gains = jnp.transpose(gain_ref[...])
        for j in range(model // HD):
            rows = slice(j * HD, (j + 1) * HD)
            at = 0
            for ref, width in zip(weight_refs, widths):
                part = ref[0, rows, :].astype(jnp.float32) * gains[:, j : j + 1]
                scaled_ref[rows, at : at + width] = part.astype(jnp.bfloat16)
                at += width

    tokens = tokens_ref[...]
    values = tokens.astype(jnp.float32)
    inverse = lax.rsqrt(jnp.mean(values * values, axis=-1, keepdims=True) + 1e-05)
    result = jnp.dot(tokens, scaled_ref[...], preferred_element_type=jnp.float32) * inverse
    result = result.astype(jnp.bfloat16)
    at = 0
    for ref in out_refs:
        width = ref.shape[2]
        ref[...] = result[:, at : at + width].reshape(ref.shape)
        at += width


def project(tokens, gain, weights, columns, outs, limit):
    rows, model = tokens.shape
    tiles, count = rows // TILE, BLOCK // TILE
    widths = [n * HD for _, _, n in columns]
    return pl.pallas_call(
        functools.partial(project_kernel, widths=widths, scales=len(outs)),
        grid=(rows // BLOCK,),
        in_specs=[
            pl.BlockSpec((BLOCK, model), lambda i: (i, 0)),
            pl.BlockSpec(gain.shape, lambda i: (0, 0)),
        ]
        + [
            pl.BlockSpec((1, model, n * HD), lambda i, c=c, b=b: (c, 0, b), pipeline_mode=pl.Buffered(1))
            for c, b, n in columns
        ],
        out_specs=[pl.BlockSpec((count, TILE, width), lambda i: (i, 0, 0)) for width in outs],
        out_shape=[jax.ShapeDtypeStruct((tiles, TILE, width), jnp.bfloat16) for width in outs],
        scratch_shapes=[pltpu.VMEM((model, sum(widths)), jnp.bfloat16)],
        compiler_params=pltpu.CompilerParams(vmem_limit_bytes=limit),
        name="project",
    )(tokens, gain, *([weights] * len(columns)))


def dispatch_kernel(me_ref, chosen_ref, held_ref, *rest, shifts):
    send_refs, staged, semaphores = rest[:-2], rest[-2], rest[-1]
    copies = []
    for p, shift in enumerate(shifts):
        target = shifted(me_ref[0], shift)
        for k in range(CAP):
            staged[p, k] = held_ref[chosen_ref[k, target]]
        copies.append(pltpu.make_async_copy(staged.at[p], send_refs[p], semaphores.at[p]))
        copies[-1].start()
    for copy in copies:
        copy.wait()


def dispatch(me, chosen, held, shifts):
    shape = (CAP,) + held.shape[1:]
    smem = pl.BlockSpec(memory_space=pltpu.SMEM)
    return pl.pallas_call(
        functools.partial(dispatch_kernel, shifts=shifts),
        in_specs=[smem, smem, pl.BlockSpec(memory_space=pltpu.VMEM)],
        out_specs=[pl.BlockSpec(memory_space=pltpu.HBM)] * len(shifts),
        out_shape=[jax.ShapeDtypeStruct(shape, held.dtype)] * len(shifts),
        scratch_shapes=[
            pltpu.VMEM((len(shifts),) + shape, held.dtype),
            pltpu.SemaphoreType.DMA((len(shifts),)),
        ],
        compiler_params=pltpu.CompilerParams(vmem_limit_bytes=MOST),
        name="dispatch",
    )(me, chosen, held)


def attend_kernel(first_ref, source_ref, queries_ref, own_ref, *rest, tiles, heads, pairs, steps):
    count = len(steps)
    incoming_refs, out_refs, held, semaphores = rest[: -2 - count], rest[-2 - count : -2], rest[-2], rest[-1]
    copies = []
    for p, shift in enumerate(SHIFTS):
        copies.append(
            pltpu.make_async_copy(incoming_refs[p], held.at[pl.ds(shift * CAP, CAP)], semaphores.at[p])
        )
        copies[-1].start()
    for copy in copies:
        copy.wait()
    scale = 1.0 / math.sqrt(HD) * math.log2(math.e)
    share = tiles // pairs
    for start in range(0, share * count, GROUP):
        block = (first_ref[1] + steps[start // share]) % pairs * share
        group = [block + (start + g) % share for g in range(GROUP)]
        blocks = [
            [own_ref.at[i]] + [held.at[source_ref[j, first_ref[0] + i]] for j in range(1, KT)] for i in group
        ]
        work = [(g, h) for g in range(GROUP) for h in range(heads)]
        scores = [
            [
                lax.dot_general(
                    queries_ref[group[g], :, h * HD : (h + 1) * HD],
                    b[:, h * HD : (h + 1) * HD],
                    (((1,), (1,)), ((), ())),
                    preferred_element_type=jnp.float32,
                )
                for b in blocks[g]
            ]
            for g, h in work
        ]
        highest = [jnp.max(functools.reduce(jnp.maximum, s), axis=-1, keepdims=True) * scale for s in scores]
        exponents = [[jnp.exp2(x * scale - m) for x in s] for s, m in zip(scores, highest)]
        totals = [jnp.sum(functools.reduce(jnp.add, e), axis=-1, keepdims=True) for e in exponents]
        for (g, h), e, total in zip(work, exponents, totals):
            weights = jnp.concatenate([x.astype(jnp.bfloat16) for x in e], axis=1)
            upper = slice((heads + h) * HD, (heads + h + 1) * HD)
            values = jnp.concatenate([b[:, upper] for b in blocks[g]], axis=0)
            attended = jnp.dot(weights, values, preferred_element_type=jnp.float32)
            row = (start + g) % share * TILE
            out_refs[start // share][row : row + TILE, h * HD : (h + 1) * HD] = (
                attended * (1.0 / total)
            ).astype(jnp.bfloat16)


def attend(first, source, queries, own, incoming, pairs, steps):
    tiles = own.shape[0]
    vmem, smem = pl.BlockSpec(memory_space=pltpu.VMEM), pl.BlockSpec(memory_space=pltpu.SMEM)
    return pl.pallas_call(
        functools.partial(attend_kernel, tiles=tiles, heads=queries.shape[2] // HD, pairs=pairs, steps=steps),
        in_specs=[smem, smem, vmem, vmem] + [pl.BlockSpec(memory_space=pl.ANY)] * len(incoming),
        out_specs=[vmem] * len(steps),
        out_shape=[jax.ShapeDtypeStruct((tiles * TILE // pairs, queries.shape[2]), jnp.bfloat16)] * len(steps),
        scratch_shapes=[
            pltpu.VMEM((SIDE * SIDE * CAP,) + own.shape[1:], jnp.bfloat16),
            pltpu.SemaphoreType.DMA((len(incoming),)),
        ],
        compiler_params=pltpu.CompilerParams(vmem_limit_bytes=VMEM),
        name="attend",
    )(first, source, queries, own, *incoming)


def mix_kernel(half_ref, *refs):
    out_ref, count = refs[-1], len(refs) // 2
    parts = [
        jnp.dot(left[0], right[...], preferred_element_type=jnp.float32)
        for left, right in zip(refs[:count], refs[count:])
    ]
    out_ref[...] = functools.reduce(jnp.add, parts).astype(out_ref.dtype)


def mix(half, attended, weights, dtype):
    rows, width = attended[0].shape
    model = weights[0].shape[1]
    return pl.pallas_call(
        mix_kernel,
        grid_spec=pltpu.PrefetchScalarGridSpec(
            num_scalar_prefetch=1,
            grid=(model // COLUMNS,),
            in_specs=[pl.BlockSpec((1, rows // 2, width), lambda i, h: (h[0], 0, 0))] * len(attended)
            + [pl.BlockSpec((width, COLUMNS), lambda i, h: (0, i))] * len(weights),
            out_specs=pl.BlockSpec((rows // 2, COLUMNS), lambda i, h: (0, i)),
        ),
        out_shape=jax.ShapeDtypeStruct((rows // 2, model), dtype),
        compiler_params=pltpu.CompilerParams(vmem_limit_bytes=LEAST),
        name="mix",
    )(half, *[x.reshape(2, rows // 2, width) for x in attended], *weights)


def body(tokens, norm_gain, in_weight, out_weight, pattern):
    shards = lax.axis_size("seq")
    groups = lax.axis_size("head")
    myself = lax.axis_index("seq")
    row_count, model = tokens.shape
    tiles = row_count // TILE
    width = in_weight.shape[2]
    heads = width // HD
    me = jnp.reshape(myself, (1,)).astype(jnp.int32)

    pairs = groups // 2
    place = lax.axis_index("head")
    pair, core = place // 2, place % 2

    def along(x, shift):
        return lax.ppermute(x, "head", [(s, (s // 2 + shift) % pairs * 2 + s % 2) for s in range(groups)])

    chosen, source = pl.pallas_call(
        functools.partial(tables_kernel, shards=shards, tiles=tiles),
        in_specs=[pl.BlockSpec(memory_space=pltpu.SMEM), pl.BlockSpec(memory_space=pltpu.VMEM)],
        out_shape=[
            jax.ShapeDtypeStruct((8, 128), jnp.int32),
            jax.ShapeDtypeStruct((KT, shards * tiles), jnp.int32),
        ],
        name="tables",
    )(me, pattern.T)

    gain = norm_gain.reshape(model // HD, HD)
    weights = in_weight.transpose(1, 0, 2)
    mixers = {shift: along(out_weight, shift) for shift in (1, 3)}
    (own,) = project(tokens, gain, weights, [(1, 0, heads), (2, 0, heads)], [2 * width], MOST)
    sends = list(dispatch(me, chosen, own, SHIFTS[:FIRST]))
    held, tokens, sends = lax.optimization_barrier((own, tokens, sends))
    sends += list(dispatch(me, chosen, held, SHIFTS[FIRST:]))
    (queries,) = project(tokens, gain, weights, [(0, 0, heads)], [width], MOST)
    sends[ALONE:], mixers = lax.optimization_barrier((sends[ALONE:], mixers))
    incoming = []
    for p, shift in enumerate(SHIFTS):
        send = sends[p]
        incoming.append(lax.ppermute(send, "seq", [(s, shifted(s, shift)) for s in range(shards)]))
    late, incoming[LATE] = lax.optimization_barrier((out_weight, incoming[LATE]))
    mixers[2] = along(late, 2)
    first = jnp.stack([myself * tiles, pair]).astype(jnp.int32)
    lefts = {}
    for steps in STEPS:
        for step, block in zip(steps, attend(first, source, queries, own, incoming, pairs, steps)):
            lefts[step] = along(block, step) if step else block
    lefts = [lefts[step] for step in range(pairs)]
    rights = [out_weight] + [mixers[shift] for shift in range(1, pairs)]
    give = mix(jnp.reshape(1 - core, (1,)).astype(jnp.int32), lefts, rights, jnp.bfloat16)
    got = lax.ppermute(give, "head", [(s, s + 1 - s % 2 * 2) for s in range(groups)])
    keep = mix(jnp.reshape(core, (1,)).astype(jnp.int32), lefts, rights, jnp.float32)
    return (keep + got.astype(jnp.float32)).astype(jnp.bfloat16)


def solution(mesh):
    return jax.shard_map(
        body,
        mesh=mesh,
        in_specs=(P("seq", None), P(), P(None, None, "head"), P("head", None), P()),
        out_specs=P(("seq", "head"), None),
        check_vma=False,
    )
```

```python
import functools
import math

import jax
import jax.numpy as jnp
from jax import lax
from jax.experimental import pallas as pl
from jax.experimental.pallas import tpu as pltpu
from jax.sharding import PartitionSpec as P

HD = 128
TILE = 128
KT = 4
CAP = 4
BLOCK = 512
GROUP = 4
SIDE = 4
SHIFTS = (10, 6, 12, 14, 4, 3, 11, 1, 5, 15, 9, 7, 13, 2, 8)
FIRST = 2
STEPS = ((1, 2, 3), (0,))
ALONE = 2
LATE = 10
COLUMNS = 1024
VMEM = 60 * 1024 * 1024
MOST = 60 * 1024 * 1024
LEAST = 16 * 1024 * 1024


def shift_of(source, target):
    rows = (target // SIDE - source // SIDE + SIDE) % SIDE
    return rows * SIDE + (target % SIDE - source % SIDE + SIDE) % SIDE


def shifted(source, shift):
    return (source // SIDE + shift // SIDE) % SIDE * SIDE + (source % SIDE + shift % SIDE) % SIDE


def tables_kernel(me_ref, pattern_ref, chosen_ref, source_ref, *, shards, tiles):
    total = shards * tiles
    table = pattern_ref[...]
    owner = table // tiles
    local = table % tiles
    row = lax.broadcasted_iota(jnp.int32, (total, total), 0)
    col = lax.broadcasted_iota(jnp.int32, (total, total), 1)
    same = (row // tiles) == (col // tiles)
    every = same.astype(jnp.bfloat16)
    before = (same & (row < col)).astype(jnp.bfloat16)
    index = lax.broadcasted_iota(jnp.int32, (shards, total), 0)
    names = [(owner[c : c + 1] == index).astype(jnp.bfloat16) for c in range(1, KT)]
    dot = functools.partial(jnp.dot, preferred_element_type=jnp.float32)
    earlier = jnp.zeros((shards, total), jnp.float32)
    picked = [jnp.zeros((1, total), jnp.float32) for _ in range(CAP)]
    source_ref[0:1, :] = jnp.zeros((1, total), jnp.int32)
    for c in range(1, KT):
        here = names[c - 1]
        rank = jnp.sum(here.astype(jnp.float32) * (dot(here, before) + earlier), axis=0, keepdims=True)
        earlier = earlier + dot(here, every)
        rank = rank.astype(jnp.int32)
        mine = owner[c : c + 1] == me_ref[0]
        source_ref[c : c + 1, :] = shift_of(owner[c : c + 1], me_ref[0]) * CAP + rank
        for k in range(CAP):
            picked[k] += jnp.where(mine & (rank == k), local[c : c + 1], 0).astype(jnp.float32)
    tile_row = lax.broadcasted_iota(jnp.int32, (total, 128), 0)
    lane = lax.broadcasted_iota(jnp.int32, (total, 128), 1)
    spread = ((tile_row // tiles) == lane).astype(jnp.bfloat16)
    for k in range(CAP):
        chosen_ref[k : k + 1, :] = dot(picked[k].astype(jnp.bfloat16), spread).astype(jnp.int32)


def project_kernel(*refs, widths, scales):
    count = len(widths)
    tokens_ref, gain_ref = refs[0], refs[1]
    weight_refs = refs[2 : 2 + count]
    out_refs = refs[2 + count : 2 + count + scales]
    scaled_ref = refs[-1]
    model = scaled_ref.shape[0]
    step = pl.program_id(0)

    @pl.when(step == 0)
    def _():
        gains = jnp.transpose(gain_ref[...])
        for j in range(model // HD):
            rows = slice(j * HD, (j + 1) * HD)
            at = 0
            for ref, width in zip(weight_refs, widths):
                part = ref[0, rows, :].astype(jnp.float32) * gains[:, j : j + 1]
                scaled_ref[rows, at : at + width] = part.astype(jnp.bfloat16)
                at += width

    tokens = tokens_ref[...]
    values = tokens.astype(jnp.float32)
    inverse = lax.rsqrt(jnp.mean(values * values, axis=-1, keepdims=True) + 1e-05)
    result = jnp.dot(tokens, scaled_ref[...], preferred_element_type=jnp.float32) * inverse
    result = result.astype(jnp.bfloat16)
    at = 0
    for ref in out_refs:
        width = ref.shape[2]
        ref[...] = result[:, at : at + width].reshape(ref.shape)
        at += width


def project(tokens, gain, weights, columns, outs, limit):
    rows, model = tokens.shape
    tiles, count = rows // TILE, BLOCK // TILE
    widths = [n * HD for _, _, n in columns]
    return pl.pallas_call(
        functools.partial(project_kernel, widths=widths, scales=len(outs)),
        grid=(rows // BLOCK,),
        in_specs=[
            pl.BlockSpec((BLOCK, model), lambda i: (i, 0)),
            pl.BlockSpec(gain.shape, lambda i: (0, 0)),
        ]
        + [
            pl.BlockSpec((1, model, n * HD), lambda i, c=c, b=b: (c, 0, b), pipeline_mode=pl.Buffered(1))
            for c, b, n in columns
        ],
        out_specs=[pl.BlockSpec((count, TILE, width), lambda i: (i, 0, 0)) for width in outs],
        out_shape=[jax.ShapeDtypeStruct((tiles, TILE, width), jnp.bfloat16) for width in outs],
        scratch_shapes=[pltpu.VMEM((model, sum(widths)), jnp.bfloat16)],
        compiler_params=pltpu.CompilerParams(vmem_limit_bytes=limit),
        name="project",
    )(tokens, gain, *([weights] * len(columns)))


def dispatch_kernel(me_ref, chosen_ref, held_ref, *rest, shifts):
    send_refs, staged, semaphores = rest[:-2], rest[-2], rest[-1]
    copies = []
    for p, shift in enumerate(shifts):
        target = shifted(me_ref[0], shift)
        for k in range(CAP):
            staged[p, k] = held_ref[chosen_ref[k, target]]
        copies.append(pltpu.make_async_copy(staged.at[p], send_refs[p], semaphores.at[p]))
        copies[-1].start()
    for copy in copies:
        copy.wait()


def dispatch(me, chosen, held, shifts):
    shape = (CAP,) + held.shape[1:]
    smem = pl.BlockSpec(memory_space=pltpu.SMEM)
    return pl.pallas_call(
        functools.partial(dispatch_kernel, shifts=shifts),
        in_specs=[smem, smem, pl.BlockSpec(memory_space=pltpu.VMEM)],
        out_specs=[pl.BlockSpec(memory_space=pltpu.HBM)] * len(shifts),
        out_shape=[jax.ShapeDtypeStruct(shape, held.dtype)] * len(shifts),
        scratch_shapes=[
            pltpu.VMEM((len(shifts),) + shape, held.dtype),
            pltpu.SemaphoreType.DMA((len(shifts),)),
        ],
        compiler_params=pltpu.CompilerParams(vmem_limit_bytes=MOST),
        name="dispatch",
    )(me, chosen, held)


def attend_kernel(first_ref, source_ref, queries_ref, own_ref, *rest, tiles, heads, pairs, steps):
    count = len(steps)
    incoming_refs, out_refs, held, semaphores = rest[: -2 - count], rest[-2 - count : -2], rest[-2], rest[-1]
    copies = []
    for p, shift in enumerate(SHIFTS):
        copies.append(
            pltpu.make_async_copy(incoming_refs[p], held.at[pl.ds(shift * CAP, CAP)], semaphores.at[p])
        )
        copies[-1].start()
    for copy in copies:
        copy.wait()
    scale = 1.0 / math.sqrt(HD) * math.log2(math.e)
    share = tiles // pairs
    for start in range(0, share * count, GROUP):
        block = (first_ref[1] + steps[start // share]) % pairs * share
        group = [block + (start + g) % share for g in range(GROUP)]
        blocks = [
            [own_ref.at[i]] + [held.at[source_ref[j, first_ref[0] + i]] for j in range(1, KT)] for i in group
        ]
        work = [(g, h) for g in range(GROUP) for h in range(heads)]
        scores = [
            [
                lax.dot_general(
                    queries_ref[group[g], :, h * HD : (h + 1) * HD],
                    b[:, h * HD : (h + 1) * HD],
                    (((1,), (1,)), ((), ())),
                    preferred_element_type=jnp.float32,
                )
                for b in blocks[g]
            ]
            for g, h in work
        ]
        highest = [jnp.max(functools.reduce(jnp.maximum, s), axis=-1, keepdims=True) * scale for s in scores]
        exponents = [[jnp.exp2(x * scale - m) for x in s] for s, m in zip(scores, highest)]
        totals = [jnp.sum(functools.reduce(jnp.add, e), axis=-1, keepdims=True) for e in exponents]
        for (g, h), e, total in zip(work, exponents, totals):
            weights = jnp.concatenate([x.astype(jnp.bfloat16) for x in e], axis=1)
            upper = slice((heads + h) * HD, (heads + h + 1) * HD)
            values = jnp.concatenate([b[:, upper] for b in blocks[g]], axis=0)
            attended = jnp.dot(weights, values, preferred_element_type=jnp.float32)
            row = (start + g) % share * TILE
            out_refs[start // share][row : row + TILE, h * HD : (h + 1) * HD] = (
                attended * (1.0 / total)
            ).astype(jnp.bfloat16)


def attend(first, source, queries, own, incoming, pairs, steps):
    tiles = own.shape[0]
    vmem, smem = pl.BlockSpec(memory_space=pltpu.VMEM), pl.BlockSpec(memory_space=pltpu.SMEM)
    return pl.pallas_call(
        functools.partial(attend_kernel, tiles=tiles, heads=queries.shape[2] // HD, pairs=pairs, steps=steps),
        in_specs=[smem, smem, vmem, vmem] + [pl.BlockSpec(memory_space=pl.ANY)] * len(incoming),
        out_specs=[vmem] * len(steps),
        out_shape=[jax.ShapeDtypeStruct((tiles * TILE // pairs, queries.shape[2]), jnp.bfloat16)] * len(steps),
        scratch_shapes=[
            pltpu.VMEM((SIDE * SIDE * CAP,) + own.shape[1:], jnp.bfloat16),
            pltpu.SemaphoreType.DMA((len(incoming),)),
        ],
        compiler_params=pltpu.CompilerParams(vmem_limit_bytes=VMEM),
        name="attend",
    )(first, source, queries, own, *incoming)


def mix_kernel(half_ref, *refs):
    out_ref, count = refs[-1], len(refs) // 2
    parts = [
        jnp.dot(left[0], right[...], preferred_element_type=jnp.float32)
        for left, right in zip(refs[:count], refs[count:])
    ]
    out_ref[...] = functools.reduce(jnp.add, parts).astype(out_ref.dtype)


def mix(half, attended, weights, dtype):
    rows, width = attended[0].shape
    model = weights[0].shape[1]
    return pl.pallas_call(
        mix_kernel,
        grid_spec=pltpu.PrefetchScalarGridSpec(
            num_scalar_prefetch=1,
            grid=(model // COLUMNS,),
            in_specs=[pl.BlockSpec((1, rows // 2, width), lambda i, h: (h[0], 0, 0))] * len(attended)
            + [pl.BlockSpec((width, COLUMNS), lambda i, h: (0, i))] * len(weights),
            out_specs=pl.BlockSpec((rows // 2, COLUMNS), lambda i, h: (0, i)),
        ),
        out_shape=jax.ShapeDtypeStruct((rows // 2, model), dtype),
        compiler_params=pltpu.CompilerParams(vmem_limit_bytes=LEAST),
        name="mix",
    )(half, *[x.reshape(2, rows // 2, width) for x in attended], *weights)


def body(tokens, norm_gain, in_weight, out_weight, pattern):
    shards = lax.axis_size("seq")
    groups = lax.axis_size("head")
    myself = lax.axis_index("seq")
    row_count, model = tokens.shape
    tiles = row_count // TILE
    width = in_weight.shape[2]
    heads = width // HD
    me = jnp.reshape(myself, (1,)).astype(jnp.int32)

    pairs = groups // 2
    place = lax.axis_index("head")
    pair, core = place // 2, place % 2

    def along(x, shift):
        return lax.ppermute(x, "head", [(s, (s // 2 + shift) % pairs * 2 + s % 2) for s in range(groups)])

    chosen, source = pl.pallas_call(
        functools.partial(tables_kernel, shards=shards, tiles=tiles),
        in_specs=[pl.BlockSpec(memory_space=pltpu.SMEM), pl.BlockSpec(memory_space=pltpu.VMEM)],
        out_shape=[
            jax.ShapeDtypeStruct((8, 128), jnp.int32),
            jax.ShapeDtypeStruct((KT, shards * tiles), jnp.int32),
        ],
        name="tables",
    )(me, pattern.T)

    gain = norm_gain.reshape(model // HD, HD)
    weights = in_weight.transpose(1, 0, 2)
    mixers = {shift: along(out_weight, shift) for shift in (1, 3)}
    (own,) = project(tokens, gain, weights, [(1, 0, heads), (2, 0, heads)], [2 * width], MOST)
    sends = list(dispatch(me, chosen, own, SHIFTS[:FIRST]))
    held, tokens, sends = lax.optimization_barrier((own, tokens, sends))
    sends += list(dispatch(me, chosen, held, SHIFTS[FIRST:]))
    (queries,) = project(tokens, gain, weights, [(0, 0, heads)], [width], MOST)
    sends[ALONE:], mixers = lax.optimization_barrier((sends[ALONE:], mixers))
    incoming = []
    for p, shift in enumerate(SHIFTS):
        send = sends[p]
        incoming.append(lax.ppermute(send, "seq", [(s, shifted(s, shift)) for s in range(shards)]))
    late, incoming[LATE] = lax.optimization_barrier((out_weight, incoming[LATE]))
    mixers[2] = along(late, 2)
    first = jnp.stack([myself * tiles, pair]).astype(jnp.int32)
    lefts = {}
    for steps in STEPS:
        for step, block in zip(steps, attend(first, source, queries, own, incoming, pairs, steps)):
            lefts[step] = along(block, step) if step else block
    lefts = [lefts[step] for step in range(pairs)]
    rights = [out_weight] + [mixers[shift] for shift in range(1, pairs)]
    give = mix(jnp.reshape(1 - core, (1,)).astype(jnp.int32), lefts, rights, jnp.bfloat16)
    got = lax.ppermute(give, "head", [(s, s + 1 - s % 2 * 2) for s in range(groups)])
    keep = mix(jnp.reshape(core, (1,)).astype(jnp.int32), lefts, rights, jnp.float32)
    return (keep + got.astype(jnp.float32)).astype(jnp.bfloat16)


def solution(mesh):
    return jax.shard_map(
        body,
        mesh=mesh,
        in_specs=(P("seq", None), P(), P(None, None, "head"), P("head", None), P()),
        out_specs=P(("seq", "head"), None),
        check_vma=False,
    )
```

```python
import functools
import math

import jax
import jax.numpy as jnp
from jax import lax
from jax.experimental import pallas as pl
from jax.experimental.pallas import tpu as pltpu
from jax.sharding import PartitionSpec as P

HD = 128
TILE = 128
KT = 4
CAP = 4
BLOCK = 512
GROUP = 4
SIDE = 4
SHIFTS = (10, 6, 12, 14, 4, 3, 11, 1, 5, 15, 9, 7, 13, 2, 8)
FIRST = 2
STEPS = ((1, 2, 3), (0,))
ALONE = 2
LATE = 10
COLUMNS = 512
VMEM = 60 * 1024 * 1024
MOST = 60 * 1024 * 1024
LEAST = 16 * 1024 * 1024


def shift_of(source, target):
    rows = (target // SIDE - source // SIDE + SIDE) % SIDE
    return rows * SIDE + (target % SIDE - source % SIDE + SIDE) % SIDE


def shifted(source, shift):
    return (source // SIDE + shift // SIDE) % SIDE * SIDE + (source % SIDE + shift % SIDE) % SIDE


def tables_kernel(me_ref, pattern_ref, chosen_ref, source_ref, *, shards, tiles):
    total = shards * tiles
    table = pattern_ref[...]
    owner = table // tiles
    local = table % tiles
    row = lax.broadcasted_iota(jnp.int32, (total, total), 0)
    col = lax.broadcasted_iota(jnp.int32, (total, total), 1)
    same = (row // tiles) == (col // tiles)
    every = same.astype(jnp.bfloat16)
    before = (same & (row < col)).astype(jnp.bfloat16)
    index = lax.broadcasted_iota(jnp.int32, (shards, total), 0)
    names = [(owner[c : c + 1] == index).astype(jnp.bfloat16) for c in range(1, KT)]
    dot = functools.partial(jnp.dot, preferred_element_type=jnp.float32)
    earlier = jnp.zeros((shards, total), jnp.float32)
    picked = [jnp.zeros((1, total), jnp.float32) for _ in range(CAP)]
    source_ref[0:1, :] = jnp.zeros((1, total), jnp.int32)
    for c in range(1, KT):
        here = names[c - 1]
        rank = jnp.sum(here.astype(jnp.float32) * (dot(here, before) + earlier), axis=0, keepdims=True)
        earlier = earlier + dot(here, every)
        rank = rank.astype(jnp.int32)
        mine = owner[c : c + 1] == me_ref[0]
        source_ref[c : c + 1, :] = shift_of(owner[c : c + 1], me_ref[0]) * CAP + rank
        for k in range(CAP):
            picked[k] += jnp.where(mine & (rank == k), local[c : c + 1], 0).astype(jnp.float32)
    tile_row = lax.broadcasted_iota(jnp.int32, (total, 128), 0)
    lane = lax.broadcasted_iota(jnp.int32, (total, 128), 1)
    spread = ((tile_row // tiles) == lane).astype(jnp.bfloat16)
    for k in range(CAP):
        chosen_ref[k : k + 1, :] = dot(picked[k].astype(jnp.bfloat16), spread).astype(jnp.int32)


def project_kernel(*refs, widths, scales):
    count = len(widths)
    tokens_ref, gain_ref = refs[0], refs[1]
    weight_refs = refs[2 : 2 + count]
    out_refs = refs[2 + count : 2 + count + scales]
    scaled_ref = refs[-1]
    model = scaled_ref.shape[0]
    step = pl.program_id(0)

    @pl.when(step == 0)
    def _():
        gains = jnp.transpose(gain_ref[...])
        for j in range(model // HD):
            rows = slice(j * HD, (j + 1) * HD)
            at = 0
            for ref, width in zip(weight_refs, widths):
                part = ref[0, rows, :].astype(jnp.float32) * gains[:, j : j + 1]
                scaled_ref[rows, at : at + width] = part.astype(jnp.bfloat16)
                at += width

    tokens = tokens_ref[...]
    values = tokens.astype(jnp.float32)
    inverse = lax.rsqrt(jnp.mean(values * values, axis=-1, keepdims=True) + 1e-05)
    result = jnp.dot(tokens, scaled_ref[...], preferred_element_type=jnp.float32) * inverse
    result = result.astype(jnp.bfloat16)
    at = 0
    for ref in out_refs:
        width = ref.shape[2]
        ref[...] = result[:, at : at + width].reshape(ref.shape)
        at += width


def project(tokens, gain, weights, columns, outs, limit):
    rows, model = tokens.shape
    tiles, count = rows // TILE, BLOCK // TILE
    widths = [n * HD for _, _, n in columns]
    return pl.pallas_call(
        functools.partial(project_kernel, widths=widths, scales=len(outs)),
        grid=(rows // BLOCK,),
        in_specs=[
            pl.BlockSpec((BLOCK, model), lambda i: (i, 0)),
            pl.BlockSpec(gain.shape, lambda i: (0, 0)),
        ]
        + [
            pl.BlockSpec((1, model, n * HD), lambda i, c=c, b=b: (c, 0, b), pipeline_mode=pl.Buffered(1))
            for c, b, n in columns
        ],
        out_specs=[pl.BlockSpec((count, TILE, width), lambda i: (i, 0, 0)) for width in outs],
        out_shape=[jax.ShapeDtypeStruct((tiles, TILE, width), jnp.bfloat16) for width in outs],
        scratch_shapes=[pltpu.VMEM((model, sum(widths)), jnp.bfloat16)],
        compiler_params=pltpu.CompilerParams(vmem_limit_bytes=limit),
        name="project",
    )(tokens, gain, *([weights] * len(columns)))


def dispatch_kernel(me_ref, chosen_ref, held_ref, *rest, shifts):
    send_refs, staged, semaphores = rest[:-2], rest[-2], rest[-1]
    copies = []
    for p, shift in enumerate(shifts):
        target = shifted(me_ref[0], shift)
        for k in range(CAP):
            staged[p, k] = held_ref[chosen_ref[k, target]]
        copies.append(pltpu.make_async_copy(staged.at[p], send_refs[p], semaphores.at[p]))
        copies[-1].start()
    for copy in copies:
        copy.wait()


def dispatch(me, chosen, held, shifts):
    shape = (CAP,) + held.shape[1:]
    smem = pl.BlockSpec(memory_space=pltpu.SMEM)
    return pl.pallas_call(
        functools.partial(dispatch_kernel, shifts=shifts),
        in_specs=[smem, smem, pl.BlockSpec(memory_space=pltpu.VMEM)],
        out_specs=[pl.BlockSpec(memory_space=pltpu.HBM)] * len(shifts),
        out_shape=[jax.ShapeDtypeStruct(shape, held.dtype)] * len(shifts),
        scratch_shapes=[
            pltpu.VMEM((len(shifts),) + shape, held.dtype),
            pltpu.SemaphoreType.DMA((len(shifts),)),
        ],
        compiler_params=pltpu.CompilerParams(vmem_limit_bytes=MOST),
        name="dispatch",
    )(me, chosen, held)


def attend_kernel(first_ref, source_ref, queries_ref, own_ref, *rest, tiles, heads, pairs, steps):
    count = len(steps)
    incoming_refs, out_refs, held, semaphores = rest[: -2 - count], rest[-2 - count : -2], rest[-2], rest[-1]
    copies = []
    for p, shift in enumerate(SHIFTS):
        copies.append(
            pltpu.make_async_copy(incoming_refs[p], held.at[pl.ds(shift * CAP, CAP)], semaphores.at[p])
        )
        copies[-1].start()
    for copy in copies:
        copy.wait()
    scale = 1.0 / math.sqrt(HD) * math.log2(math.e)
    share = tiles // pairs
    for start in range(0, share * count, GROUP):
        block = (first_ref[1] + steps[start // share]) % pairs * share
        group = [block + (start + g) % share for g in range(GROUP)]
        blocks = [
            [own_ref.at[i]] + [held.at[source_ref[j, first_ref[0] + i]] for j in range(1, KT)] for i in group
        ]
        work = [(g, h) for g in range(GROUP) for h in range(heads)]
        scores = [
            [
                lax.dot_general(
                    queries_ref[group[g], :, h * HD : (h + 1) * HD],
                    b[:, h * HD : (h + 1) * HD],
                    (((1,), (1,)), ((), ())),
                    preferred_element_type=jnp.float32,
                )
                for b in blocks[g]
            ]
            for g, h in work
        ]
        highest = [jnp.max(functools.reduce(jnp.maximum, s), axis=-1, keepdims=True) * scale for s in scores]
        exponents = [[jnp.exp2(x * scale - m) for x in s] for s, m in zip(scores, highest)]
        totals = [jnp.sum(functools.reduce(jnp.add, e), axis=-1, keepdims=True) for e in exponents]
        for (g, h), e, total in zip(work, exponents, totals):
            weights = jnp.concatenate([x.astype(jnp.bfloat16) for x in e], axis=1)
            upper = slice((heads + h) * HD, (heads + h + 1) * HD)
            values = jnp.concatenate([b[:, upper] for b in blocks[g]], axis=0)
            attended = jnp.dot(weights, values, preferred_element_type=jnp.float32)
            row = (start + g) % share * TILE
            out_refs[start // share][row : row + TILE, h * HD : (h + 1) * HD] = (
                attended * (1.0 / total)
            ).astype(jnp.bfloat16)


def attend(first, source, queries, own, incoming, pairs, steps):
    tiles = own.shape[0]
    vmem, smem = pl.BlockSpec(memory_space=pltpu.VMEM), pl.BlockSpec(memory_space=pltpu.SMEM)
    return pl.pallas_call(
        functools.partial(attend_kernel, tiles=tiles, heads=queries.shape[2] // HD, pairs=pairs, steps=steps),
        in_specs=[smem, smem, vmem, vmem] + [pl.BlockSpec(memory_space=pl.ANY)] * len(incoming),
        out_specs=[vmem] * len(steps),
        out_shape=[jax.ShapeDtypeStruct((tiles * TILE // pairs, queries.shape[2]), jnp.bfloat16)] * len(steps),
        scratch_shapes=[
            pltpu.VMEM((SIDE * SIDE * CAP,) + own.shape[1:], jnp.bfloat16),
            pltpu.SemaphoreType.DMA((len(incoming),)),
        ],
        compiler_params=pltpu.CompilerParams(vmem_limit_bytes=VMEM),
        name="attend",
    )(first, source, queries, own, *incoming)


def mix_kernel(half_ref, *refs):
    out_ref, count = refs[-1], len(refs) // 2
    parts = [
        jnp.dot(left[0], right[...], preferred_element_type=jnp.float32)
        for left, right in zip(refs[:count], refs[count:])
    ]
    out_ref[...] = functools.reduce(jnp.add, parts).astype(out_ref.dtype)


def mix(half, attended, weights, dtype):
    rows, width = attended[0].shape
    model = weights[0].shape[1]
    return pl.pallas_call(
        mix_kernel,
        grid_spec=pltpu.PrefetchScalarGridSpec(
            num_scalar_prefetch=1,
            grid=(model // COLUMNS,),
            in_specs=[pl.BlockSpec((1, rows // 2, width), lambda i, h: (h[0], 0, 0))] * len(attended)
            + [pl.BlockSpec((width, COLUMNS), lambda i, h: (0, i))] * len(weights),
            out_specs=pl.BlockSpec((rows // 2, COLUMNS), lambda i, h: (0, i)),
        ),
        out_shape=jax.ShapeDtypeStruct((rows // 2, model), dtype),
        compiler_params=pltpu.CompilerParams(vmem_limit_bytes=LEAST),
        name="mix",
    )(half, *[x.reshape(2, rows // 2, width) for x in attended], *weights)


def body(tokens, norm_gain, in_weight, out_weight, pattern):
    shards = lax.axis_size("seq")
    groups = lax.axis_size("head")
    myself = lax.axis_index("seq")
    row_count, model = tokens.shape
    tiles = row_count // TILE
    width = in_weight.shape[2]
    heads = width // HD
    me = jnp.reshape(myself, (1,)).astype(jnp.int32)

    pairs = groups // 2
    place = lax.axis_index("head")
    pair, core = place // 2, place % 2

    def along(x, shift):
        return lax.ppermute(x, "head", [(s, (s // 2 + shift) % pairs * 2 + s % 2) for s in range(groups)])

    chosen, source = pl.pallas_call(
        functools.partial(tables_kernel, shards=shards, tiles=tiles),
        in_specs=[pl.BlockSpec(memory_space=pltpu.SMEM), pl.BlockSpec(memory_space=pltpu.VMEM)],
        out_shape=[
            jax.ShapeDtypeStruct((8, 128), jnp.int32),
            jax.ShapeDtypeStruct((KT, shards * tiles), jnp.int32),
        ],
        name="tables",
    )(me, pattern.T)

    gain = norm_gain.reshape(model // HD, HD)
    weights = in_weight.transpose(1, 0, 2)
    mixers = {shift: along(out_weight, shift) for shift in (1, 3)}
    (own,) = project(tokens, gain, weights, [(1, 0, heads), (2, 0, heads)], [2 * width], MOST)
    sends = list(dispatch(me, chosen, own, SHIFTS[:FIRST]))
    held, tokens, sends = lax.optimization_barrier((own, tokens, sends))
    sends += list(dispatch(me, chosen, held, SHIFTS[FIRST:]))
    (queries,) = project(tokens, gain, weights, [(0, 0, heads)], [width], MOST)
    sends[ALONE:], mixers = lax.optimization_barrier((sends[ALONE:], mixers))
    incoming = []
    for p, shift in enumerate(SHIFTS):
        send = sends[p]
        incoming.append(lax.ppermute(send, "seq", [(s, shifted(s, shift)) for s in range(shards)]))
    late, incoming[LATE] = lax.optimization_barrier((out_weight, incoming[LATE]))
    mixers[2] = along(late, 2)
    first = jnp.stack([myself * tiles, pair]).astype(jnp.int32)
    lefts = {}
    for steps in STEPS:
        for step, block in zip(steps, attend(first, source, queries, own, incoming, pairs, steps)):
            lefts[step] = along(block, step) if step else block
    lefts = [lefts[step] for step in range(pairs)]
    rights = [out_weight] + [mixers[shift] for shift in range(1, pairs)]
    give = mix(jnp.reshape(1 - core, (1,)).astype(jnp.int32), lefts, rights, jnp.bfloat16)
    got = lax.ppermute(give, "head", [(s, s + 1 - s % 2 * 2) for s in range(groups)])
    keep = mix(jnp.reshape(core, (1,)).astype(jnp.int32), lefts, rights, jnp.float32)
    return (keep + got.astype(jnp.float32)).astype(jnp.bfloat16)


def solution(mesh):
    return jax.shard_map(
        body,
        mesh=mesh,
        in_specs=(P("seq", None), P(), P(None, None, "head"), P("head", None), P()),
        out_specs=P(("seq", "head"), None),
        check_vma=False,
    )
```
